256 devices in a mesh: subj: 8 (over x, core), space: 32 (over y, z).
Axes of the slice: x: 4, y: 4, z: 8, core: 2. Of those that a mesh axis runs over, the one named last changes fastest.
Arguments:
- images: bfloat16 [16, 2048, 16, 128], P('subj', 'space'), may hold values from -6 to 6
- velocity: float32 [3, 16, 2048, 16, 128], P(None, 'subj', 'space'), may hold values from -4 to 4
- weights: bfloat16 [3, 16, 2048, 16, 128], P(None, 'subj', 'space'), may hold values from 0 to 1
- template: float32 [2048, 16, 128], P('space', 'subj'), may hold values from -6 to 6
- owners: int32 [16, 2048, 1], P('subj', 'space'), may hold values from 0 to 31; in each aligned block of 64 rows (0 to 63, 64 to 127, ..., all dimensions but the last counted through in order) at most 4 rows name the same one
- local_rows: int32 [16, 2048], P('subj', 'space'), may hold values from 0 to 63
- tile_counts: int32 [16, 32], P('subj', 'space'), may hold values from 32 to 64
Outputs:
- new_velocity: float32 [3, 16, 2048, 16, 128], P(None, 'subj', 'space')
- new_template: float32 [2048, 16, 128], P('space', 'subj')
The draws below stay inside these ranges and needn't reach their ends.
Inputs may be any that keep to these rules, and one draw needn't show every extreme that they name: `owners`: for each subject and each aligned block of 64 tiles, no value appears more than 4 times, and some value appears exactly 4 times.
All inputs are finite; a program needn't handle non-finite values.
Results may differ from the reference program's by a relative error of at most 0.0006.
Values may be sent and summed in bfloat16 or wider, within the bound.
A program may use at most 64 MiB of HBM per device.

```python
import math
import jax
import jax.numpy as jnp
import numpy as np
from jax import lax

BX = 4
BY = 4
BZ = 128
PLANE = 16
SUBJ = 16
ROWS_DEV = 64
ROWS = 2048
CAP = 4
ITERS = 2
N_SPACE = 32


def place_ends(values, rng, least, high):
    longest = values.shape.index(max(values.shape))
    spots = []
    for shift in (0, 1):
        where = [jax.random.randint(jax.random.fold_in(rng, axis), (), 0, length) for axis, length in enumerate(values.shape)]
        where[longest] = (where[longest] + shift) % values.shape[longest]
        spots.append(tuple(where))
    return values.at[spots[0]].set(least).at[spots[1]].set(high)


def levels(key, dims, shards, low, largest):
    gain = 1.0
    for dim, blocks in shards:
        draws = jax.random.uniform(jax.random.fold_in(jax.random.fold_in(key, 6), dim), (blocks,), jnp.float32, low / len(shards), largest / len(shards))
        gain = gain * jnp.repeat(jnp.exp(draws), dims[dim] // blocks).reshape((-1,) + (1,) * (len(dims) - 1 - dim))
    return gain


def shared_out(own_key, own, number, rows, count, top, most, slope):
    sequence = jax.random.permutation(own_key, count)
    packed, common = load_shares(count, rows * top, most, slope, True), load_shares(count, rows * top, most, slope, False)
    places = jnp.arange(count)

    def named(sizes, rotation):
        used = int((sizes > 0).sum())
        fixed = max(1, used // 4)
        passed = fixed + (places - fixed + rotation * (used - fixed)) % max(1, count - fixed)
        return jnp.zeros((count,), jnp.int32).at[sequence[jnp.where(places < fixed, places, passed)]].set(jnp.asarray(sizes, jnp.int32))

    sizes = jnp.where(number % 4 == 0, named(packed, number // 4), named(common, number - number // 4 - 1))
    mixed = jax.random.permutation(jax.random.fold_in(own, 3), count)
    giver, taker = mixed[0:count // 2 * 2:2], mixed[1:count // 2 * 2:2]
    room = jnp.minimum(sizes[giver] - 1, most - sizes[taker]) // 2
    room = jnp.where((giver == sequence[0]) | (taker == sequence[0]) | (sizes[taker] == 0), 0, jnp.maximum(room, 0))
    passed = jax.random.randint(jax.random.fold_in(own, 4), (count // 2,), 0, 1 << 20) % (room + 1)
    sizes = sizes.at[giver].add(-passed).at[taker].add(passed)
    labels = jnp.searchsorted(jnp.cumsum(sizes), jnp.arange(rows * top), side="right").astype(jnp.int32)
    grid = labels.reshape(top, rows).T
    grid = grid[jax.random.permutation(jax.random.fold_in(own, 1), rows)]
    rotation = jax.random.randint(jax.random.fold_in(own, 2), (rows, 1), 0, top)
    return jnp.take_along_axis(grid, (jnp.arange(top)[None, :] + rotation) % top, axis=1)


def load_shares(count, total, bound, lean, full):
    weights = [(1 << 20) // math.isqrt(standing ** lean) + 1 for standing in range(1, count + 1)]
    largest = bound if full else min(bound, max(-(-total // count), total * weights[0] // sum(weights)))
    least = 1 if total - largest >= count - 1 else 0
    given, spare = [largest] + [least] * (count - 1), total - largest - least * (count - 1)
    while spare > 0:
        movable = [i for i in range(1, count) if given[i] < largest] or [i for i in range(1, count) if given[i] < bound]
        whole, left = sum([weights[i] for i in movable]), spare
        for i in movable:
            more = min(bound - given[i], max(1, left * weights[i] // whole), spare)
            given[i] = given[i] + more
            spare = spare - more
    return np.array(given)


def bell_draw(own_key, dims, scale, limit, split=(), kind=jnp.bfloat16):
    gain = levels(own_key, dims, split, -0.22, 0.18) if split else 1.0
    values = jax.random.normal(own_key, dims, jnp.float32) * scale * gain
    return jnp.minimum(jnp.maximum(values, -limit), limit).astype(kind)


def setup_inputs(seed: int = 0) -> dict:
    key_list = jax.random.split(jax.random.key(seed), 8)
    images = bell_draw(key_list[0], (SUBJ, ROWS, PLANE, BZ), 1.0, 6.0, ((0, 8), (1, 32)))
    velocity = bell_draw(key_list[1], (3, SUBJ, ROWS, PLANE, BZ), 0.3, 4.0, ((1, 8), (2, 32)), jnp.float32)
    weights = jnp.clip(1.0 * jax.random.uniform(key_list[2], (3, SUBJ, ROWS, PLANE, BZ), jnp.float32) ** levels(key_list[2], (3, SUBJ, ROWS, PLANE, BZ), ((1, 8), (2, 32)), -0.2, 0.2), 0.0, 1.0).astype(jnp.bfloat16)
    template = bell_draw(key_list[3], (ROWS, PLANE, BZ), 1.0, 6.0, ((0, 32), (1, 8)), jnp.float32)
    owners_keys = jax.random.split(jax.random.fold_in(key_list[4], 1), SUBJ * ROWS // ROWS_DEV)
    owners_turns = jax.random.permutation(jax.random.fold_in(key_list[4], 3), SUBJ * ROWS // ROWS_DEV)
    owners = jax.vmap(lambda own, number: shared_out(jax.random.fold_in(key_list[4], 2), own, number, ROWS_DEV, N_SPACE, 1, CAP, 1))(owners_keys, owners_turns).reshape((SUBJ, ROWS, 1))
    local_rows = place_ends(jax.random.randint(key_list[5], (SUBJ, ROWS), 0, ROWS_DEV), jax.random.fold_in(key_list[5], 1), 0, ROWS_DEV - 1).astype(jnp.int32)
    tile_counts = place_ends(jax.random.randint(key_list[6], (SUBJ, N_SPACE), ROWS_DEV // 2, ROWS_DEV + 1), jax.random.fold_in(key_list[6], 1), ROWS_DEV // 2, ROWS_DEV).astype(jnp.int32)
    return {"images": images, "velocity": velocity, "weights": weights, "template": template, "owners": owners, "local_rows": local_rows, "tile_counts": tile_counts}


ridge = 0.25


def shift_up(field, axis):
    body_part = lax.slice_in_dim(field, 1, field.shape[axis], axis=axis)
    edge = jnp.zeros_like(lax.slice_in_dim(field, 0, 1, axis=axis))
    return jnp.concatenate([body_part, edge], axis)


def shift_down(field, axis):
    body_part = lax.slice_in_dim(field, 0, field.shape[axis] - 1, axis=axis)
    edge = jnp.zeros_like(lax.slice_in_dim(field, 0, 1, axis=axis))
    return jnp.concatenate([edge, body_part], axis)


def trilinear(brick, frac_x, frac_y, frac_z):
    depth = brick.ndim
    total = jnp.zeros_like(brick)
    for offset_x in (0, 1):
        moved_x = brick if offset_x == 0 else shift_up(brick, depth - 3)
        weight_x = (1.0 - frac_x) if offset_x == 0 else frac_x
        for offset_y in (0, 1):
            moved = moved_x if offset_y == 0 else shift_up(moved_x, depth - 2)
            weight_y = (1.0 - frac_y) if offset_y == 0 else frac_y
            along_z = (1.0 - frac_z) * moved + frac_z * shift_up(moved, depth - 1)
            total = total + weight_x * weight_y * along_z
    return total


def gradients(field):
    depth = field.ndim
    return jnp.stack([0.5 * (shift_up(field, depth - 3 + offset) - shift_down(field, depth - 3 + offset)) for offset in range(3)])


def smooth_z(field):
    depth = field.ndim
    return 0.25 * shift_down(field, depth - 1) + 0.5 * field + 0.25 * shift_up(field, depth - 1)


def predict(warped, grads, field):
    return warped + (grads[0] * field[0] + grads[1] * field[1]) + grads[2] * field[2]


def reference(images, velocity, weights, template, owners, local_rows, tile_counts):
    rows = ROWS_DEV * N_SPACE
    source = (owners[:, :, 0] * ROWS_DEV + local_rows).astype(jnp.int32)
    tiles = jnp.arange(rows, dtype=jnp.int32)
    counts = jnp.take(tile_counts, tiles // ROWS_DEV, axis=1)
    first = counts // 2
    position = (tiles % ROWS_DEV)[None, :]
    live = ((position < first) | (position >= ROWS_DEV - (counts - first))).astype(jnp.float32)
    fractions = jnp.moveaxis(weights, 1, 0)

    def warp_subject(items):
        image, src, alive, frac = items
        brick = image[src].astype(jnp.float32).reshape(rows, BX, BY, BZ)
        frac = frac.astype(jnp.float32).reshape(3, rows, BX, BY, BZ)
        warped = trilinear(brick, frac[0], frac[1], frac[2]) * alive[:, None, None, None]
        return warped, gradients(warped)

    warped, grads = lax.map(warp_subject, (images, source, live, fractions))
    grads = jnp.moveaxis(grads, 1, 0)
    field = velocity.reshape(3, SUBJ, rows, BX, BY, BZ)
    current = template.reshape(rows, BX, BY, BZ)
    for step in range(ITERS):
        predicted = predict(warped, grads, field)
        ratio = (predicted - current[None]) / (grads[0] * grads[0] + grads[1] * grads[1] + grads[2] * grads[2] + ridge)
        update = grads * ratio[None]
        rowwise = 0.25 * shift_down(update, 2) + 0.5 * update + 0.25 * shift_up(update, 2)
        field = field - smooth_z(rowwise)
        current = jnp.sum(predict(warped, grads, field), axis=0) / SUBJ
    return field.reshape(3, SUBJ, rows, PLANE, BZ), current.reshape(rows, PLANE, BZ)
```

```python
import functools

import jax
import jax.numpy as jnp
from jax import lax
from jax.experimental import pallas as pl
from jax.experimental.pallas import tpu as pltpu
from jax.sharding import PartitionSpec as P

MESH = pl.DeviceIdType.MESH
F32 = jnp.float32
I32 = jnp.int32
PLANE = 16
LANES = 128


def kernel(
    nj, ny, nz, rows, cap,
    img_h, vel_h, wts_h, tin_ref, own_ref, loc_ref, cnt_ref,
    out_h, tout_ref,
    img, wts, f, sendb, recvb0, recvb1, warp, g, q, r, pr, cur0, cur1, total,
    tsend, trecv, req, rreq, slot_v, rreq_s, slot_s, edge, halo,
    part, crecv, xsend, xrecv, fsend, frecv, fx, fxrecv,
    in_sem, out_sem, tsend_sem, trecv_sem, qsend_sem, qrecv_sem, loc_sem,
    bsend_sem, brecv_sem, hsend_sem, hrecv_sem,
    csend_sem, crecv_sem, xsend_sem, xrecv_sem, gsend_sem, grecv_sem,
    asend_sem, arecv_sem, fsend_sem, frecv_sem, ysend_sem, yrecv_sem,
):
    ns = ny * nz
    nx = nj // 2
    pd = PLANE // nj
    sj = lax.axis_index("subj")
    sp = lax.axis_index("space")
    x, c = sj // 2, sj % 2
    y, z = sp // nz, sp % nz
    mate = x * 2 + (1 - c)
    recvb = (recvb0, recvb1)
    half = rows // 2
    piece = rows // nj

    def peer(j):
        dy, zi = j % ny, j // ny
        dz = jnp.where(zi % 2 == 1, (zi + 1) // 2, nz - zi // 2)
        return ((y + dy) % ny) * nz + (z + dz) % nz

    img_in = pltpu.make_async_copy(img_h, img, in_sem.at[0])
    img_in.start()
    wts_in = pltpu.make_async_copy(wts_h, wts, in_sem.at[1])
    wts_in.start()
    vel_in = pltpu.make_async_copy(vel_h, f, in_sem.at[2])
    vel_in.start()

    barrier = pltpu.get_barrier_semaphore()

    def greet(j, carry):
        pl.semaphore_signal(barrier, inc=1, device_id=(sj, peer(j)), device_id_type=MESH)
        return carry

    def greet_subj(i, carry):
        pl.semaphore_signal(barrier, inc=1, device_id=((sj + i) % nj, sp), device_id_type=MESH)
        return carry

    lax.fori_loop(1, ns, greet, 0)
    lax.fori_loop(1, nj, greet_subj, 0)

    for p in range(pd):
        tsend[p] = tin_ref[pl.ds(p, rows, stride=pd), :]

    i0 = lax.broadcasted_iota(I32, (rows, rows), 0)
    i1 = lax.broadcasted_iota(I32, (rows, rows), 1)
    who = lax.broadcasted_iota(I32, (ns, rows), 0)
    lane = lax.broadcasted_iota(I32, (ns, LANES), 1)
    asked = jnp.zeros((ns, LANES), I32)
    slot_v[...] = jnp.zeros_like(slot_v)
    for s in range(2):
        count = cnt_ref[0, s]
        first = count // 2
        last = rows - (count - first)
        row = own_ref[s]
        col = jnp.sum(jnp.where(i0 == i1, row, 0), axis=1, keepdims=True)
        alive0 = (i0 < first) | (i0 >= last)
        hit = (col == row) & (i0 < i1) & alive0
        before = jnp.sum(jnp.where(hit, 1, 0), axis=0, keepdims=True)
        t1 = i1[0:1, :]
        alive1 = (t1 < first) | (t1 >= last)
        slot = jnp.where(alive1, row * cap + before, 0)
        slot_v[s, :, 0:rows] = slot
        place = jnp.where(alive1, before, cap)
        for k in range(cap):
            mine = (row == who) & (place == k)
            column = jnp.sum(jnp.where(mine, loc_ref[s : s + 1, :], 0), axis=1, keepdims=True)
            asked = asked + jnp.where(lane == s * cap + k, column, 0)
    for d in range(ns):
        req[d] = asked[d : d + 1, :]
    slots_in = pltpu.make_async_copy(slot_v, slot_s, loc_sem.at[0])
    slots_in.start()

    pl.semaphore_wait(barrier, ns - 1 + nj - 1)

    def ask(j):
        d = peer(j)
        return pltpu.make_async_remote_copy(
            src_ref=req.at[d], dst_ref=rreq.at[sp],
            send_sem=qsend_sem.at[j], recv_sem=qrecv_sem.at[sp],
            device_id=(sj, d), device_id_type=MESH,
        )

    def asked_by(d):
        return pltpu.make_async_remote_copy(
            src_ref=req.at[d], dst_ref=rreq.at[d],
            send_sem=qsend_sem.at[0], recv_sem=qrecv_sem.at[d],
            device_id=(sj, sp), device_id_type=MESH,
        )

    def start_ask(j, carry):
        ask(j).start()
        return carry

    lax.fori_loop(1, ns, start_ask, 0)
    own_ask = pltpu.make_async_copy(req.at[sp], rreq.at[sp], loc_sem.at[1])
    own_ask.start()

    def plane_copy(i):
        return pltpu.make_async_remote_copy(
            src_ref=tsend, dst_ref=trecv.at[sj],
            send_sem=tsend_sem.at[i], recv_sem=trecv_sem.at[sj],
            device_id=((sj + i) % nj, sp), device_id_type=MESH,
        )

    def start_planes(i, carry):
        plane_copy(i).start()
        return carry

    lax.fori_loop(1, nj, start_planes, 0)

    def wait_ask(j, carry):
        asked_by(peer(j)).wait_recv()
        return carry

    own_ask.wait()
    lax.fori_loop(1, ns, wait_ask, 0)
    rreq_in = pltpu.make_async_copy(rreq, rreq_s, loc_sem.at[2])
    rreq_in.start()
    img_in.wait()
    rreq_in.wait()

    def brick(s, j):
        d = peer(j)
        return pltpu.make_async_remote_copy(
            src_ref=sendb.at[s, pl.ds(d * cap, cap)], dst_ref=recvb[s].at[pl.ds(sp * cap, cap)],
            send_sem=bsend_sem.at[s, j], recv_sem=brecv_sem.at[s, sp],
            device_id=(sj, d), device_id_type=MESH,
        )

    def brick_from(s, d):
        return pltpu.make_async_remote_copy(
            src_ref=sendb.at[s, pl.ds(d * cap, cap)], dst_ref=recvb[s].at[pl.ds(d * cap, cap)],
            send_sem=bsend_sem.at[s, 0], recv_sem=brecv_sem.at[s, d],
            device_id=(sj, sp), device_id_type=MESH,
        )

    for s in range(2):

        def gather(j, carry):
            d = peer(j)
            for k in range(cap):
                sendb[s, d * cap + k] = img[s, rreq_s[d, 0, s * cap + k]]

            @pl.when(j >= 2)
            def _():
                brick(s, j - 1).start()

            return carry

        lax.fori_loop(1, ns, gather, 0)
        for k in range(cap):
            recvb[s][sp * cap + k] = img[s, rreq_s[sp, 0, s * cap + k]]
        brick(s, ns - 1).start()

    def wait_planes(i, carry):
        other = (sj + i) % nj
        pltpu.make_async_remote_copy(
            src_ref=tsend, dst_ref=trecv.at[other],
            send_sem=tsend_sem.at[0], recv_sem=trecv_sem.at[other],
            device_id=(sj, sp), device_id_type=MESH,
        ).wait_recv()
        return carry

    lax.fori_loop(1, nj, wait_planes, 0)
    trecv[sj] = tsend[...]
    for j in range(nj):
        for p in range(pd):
            cur0[pl.ds(j * pd + p, rows, stride=PLANE), :] = trecv[j, p]

    @pl.when(sp == 0)
    def _():
        halo[:, 0] = jnp.zeros_like(halo[:, 0])

    @pl.when(sp == ns - 1)
    def _():
        halo[:, 1] = jnp.zeros_like(halo[:, 1])

    wts_in.wait()
    vel_in.wait()
    slots_in.wait()

    lanes = lax.broadcasted_iota(I32, (8, LANES), 1)
    subs = lax.broadcasted_iota(I32, (8, LANES), 0)
    low = subs < 4
    y_top = subs % 4 == 3
    y_bot = subs % 4 == 0
    z_top = lanes == LANES - 1
    z_bot = lanes == 0

    def up_z(v):
        return jnp.where(z_top, 0.0, pltpu.roll(v, LANES - 1, 1))

    def down_z(v):
        return jnp.where(z_bot, 0.0, pltpu.roll(v, 1, 1))

    def up_y(v):
        return jnp.where(y_top, 0.0, pltpu.roll(v, 7, 0))

    def down_y(v):
        return jnp.where(y_bot, 0.0, pltpu.roll(v, 1, 0))

    def up_x(pair):
        a, b = [pltpu.roll(v, 4, 0) for v in pair]
        return [jnp.where(low, a, b), jnp.where(low, b, 0.0)]

    def pair_of(value):
        return [value[0:8], value[8:16]]

    def put(ref, index, pair):
        ref[index + (slice(0, 8),)] = pair[0]
        ref[index + (slice(8, 16),)] = pair[1]

    both = (0, 1)

    for s in range(2):

        def arrived(j, carry):
            brick_from(s, peer(j)).wait_recv()
            return carry

        lax.fori_loop(1, ns, arrived, 0)
        count = cnt_ref[0, s]
        first = count // 2
        last = rows - (count - first)

        def warp_tile(t, carry):
            b00 = pair_of(recvb[s][slot_s[s, 0, t]].astype(F32))
            wx, wy, wz = [pair_of(wts[a, s, t].astype(F32)) for a in range(3)]
            live = jnp.where((t < first) | (t >= last), 1.0, 0.0).astype(F32)
            d00 = [up_z(v) - v for v in b00]
            b01, d01 = [up_y(v) for v in b00], [up_y(v) for v in d00]
            b10, d10 = up_x(b00), up_x(d00)
            b11, d11 = up_x(b01), up_x(d01)
            w = []
            for i in both:
                l00 = b00[i] + wz[i] * d00[i]
                l01 = b01[i] + wz[i] * d01[i]
                l10 = b10[i] + wz[i] * d10[i]
                l11 = b11[i] + wz[i] * d11[i]
                m0 = l00 + wy[i] * (l01 - l00)
                m1 = l10 + wy[i] * (l11 - l10)
                w.append((m0 + wx[i] * (m1 - m0)) * live)
            h = [0.5 * v for v in w]
            ra, rb = [pltpu.roll(v, 4, 0) for v in h]
            mid = jnp.where(low, ra, rb)
            gx = [mid - jnp.where(low, 0.0, ra), jnp.where(low, rb, 0.0) - mid]
            gy = [up_y(v) - down_y(v) for v in h]
            gz = [up_z(v) - down_z(v) for v in h]
            here = pl.multiple_of(t * PLANE, PLANE)
            now = pair_of(cur0[pl.ds(here, PLANE), :])
            fx0, fy0, fz0 = [pair_of(f[a, s, t]) for a in range(3)]
            qq, rr = [], []
            for i in both:
                sq = gx[i] * gx[i] + gy[i] * gy[i] + gz[i] * gz[i]
                inverse = 1.0 / (16.0 * sq + 4.0)
                pred = w[i] + (gx[i] * fx0[i] + gy[i] * fy0[i]) + gz[i] * fz0[i]
                qq.append(inverse)
                rr.append((pred - now[i]) * inverse)
            put(warp, (s, t), w)
            put(g, (0, s, t), gx)
            put(g, (1, s, t), gy)
            put(g, (2, s, t), gz)
            put(q, (s, t), qq)
            put(r, (s, t), rr)
            return carry

        lax.fori_loop(0, rows, warp_tile, 0)

    def first_ratio(s, t):
        return pair_of(r[s, t])

    def second_ratio(s, t):
        here = pl.multiple_of(t * PLANE, PLANE)
        now = pair_of(cur1[pl.ds(here, PLANE), :])
        p1 = pair_of(pr[s, t])
        qq = pair_of(q[s, t])
        return [(p1[i] - now[i]) * qq[i] for i in both]

    def edge_copy(it, side):
        d = sp - 1 if side == 0 else sp + 1
        return pltpu.make_async_remote_copy(
            src_ref=edge.at[it, side], dst_ref=halo.at[it, 1 - side],
            send_sem=hsend_sem.at[it, side], recv_sem=hrecv_sem.at[it, 1 - side],
            device_id=(sj, d), device_id_type=MESH,
        )

    def halo_in(it, side):
        return pltpu.make_async_remote_copy(
            src_ref=edge.at[it, side], dst_ref=halo.at[it, side],
            send_sem=hsend_sem.at[it, side], recv_sem=hrecv_sem.at[it, side],
            device_id=(sj, sp), device_id_type=MESH,
        )

    def iterate(it):
        ratio = first_ratio if it == 0 else second_ratio

        def update(s, t):
            rr = ratio(s, t)
            out = []
            for a in range(3):
                gg = pair_of(g[a, s, t])
                out += [gg[0] * rr[0], gg[1] * rr[1]]
            return out

        for s in range(2):
            for side, t in ((0, 0), (1, rows - 1)):
                u = update(s, t)
                for a in range(3):
                    put(edge, (it, side, a, s), u[2 * a : 2 * a + 2])

        @pl.when(sp > 0)
        def _():
            edge_copy(it, 0).start()

        @pl.when(sp < ns - 1)
        def _():
            edge_copy(it, 1).start()

        def advance(s, t, v):
            new = []
            for a in range(3):
                old = pair_of(f[a, s, t])
                out = []
                for i in both:
                    value = v[2 * a + i]
                    two = value + down_z(value)
                    out.append(old[i] - (two + jnp.where(z_top, value, pltpu.roll(two, LANES - 1, 1))))
                put(f, (a, s, t), out)
                new.append(out)
            w = pair_of(warp[s, t])
            gg = [pair_of(g[a, s, t]) for a in range(3)]
            pred = [
                w[i] + (gg[0][i] * new[0][i] + gg[1][i] * new[1][i]) + gg[2][i] * new[2][i]
                for i in both
            ]
            if it == 0:
                put(pr, (s, t), pred)
            here = pl.multiple_of(t * PLANE, PLANE)
            if s == 0:
                total[pl.ds(here, 8), :] = pred[0]
                total[pl.ds(here + 8, 8), :] = pred[1]
            else:
                total[pl.ds(here, 8), :] = total[pl.ds(here, 8), :] + pred[0]
                total[pl.ds(here + 8, 8), :] = total[pl.ds(here + 8, 8), :] + pred[1]

        for s in range(2):
            u0, u1 = update(s, 0), update(s, 1)
            before = [a + b for a, b in zip(u0, u1)]

            def inner(t, carry):
                before, u = list(carry[:6]), list(carry[6:])
                after = update(s, t + 1)
                two = [a + b for a, b in zip(u, after)]
                advance(s, t, [a + b for a, b in zip(before, two)])
                return tuple(two + after)

            lax.fori_loop(1, rows - 1, inner, tuple(before + u1))

        @pl.when(sp > 0)
        def _():
            halo_in(it, 0).wait_recv()

        @pl.when(sp < ns - 1)
        def _():
            halo_in(it, 1).wait_recv()

        for s in range(2):
            for side, t, near in ((0, 0, 1), (1, rows - 1, rows - 2)):
                u, v = update(s, t), update(s, near)
                far = []
                for a in range(3):
                    far += pair_of(halo[it, side, a, s])
                advance(s, t, [(far[n] + u[n]) + (u[n] + v[n]) for n in range(6)])

    iterate(0)

    mine = c * half * PLANE
    other = (1 - c) * half * PLANE
    span = half * PLANE
    block = piece * PLANE

    to_mate = pltpu.make_async_remote_copy(
        src_ref=total.at[pl.ds(other, span)], dst_ref=crecv,
        send_sem=csend_sem.at[0], recv_sem=crecv_sem.at[0],
        device_id=(mate, sp), device_id_type=MESH,
    )
    to_mate.start()
    to_mate.wait_recv()
    xsend[...] = total[pl.ds(mine, span), :] + crecv[...]

    def chip(i):
        return (x + i) % nx

    for i in range(1, nx):
        pltpu.make_async_remote_copy(
            src_ref=xsend.at[pl.ds(chip(i) * block, block)], dst_ref=xrecv.at[x],
            send_sem=xsend_sem.at[i], recv_sem=xrecv_sem.at[x],
            device_id=(chip(i) * 2 + c, sp), device_id_type=MESH,
        ).start()
    acc = xsend[pl.ds(x * block, block), :]
    for i in range(1, nx):
        pltpu.make_async_remote_copy(
            src_ref=xrecv.at[0], dst_ref=xrecv.at[chip(i)],
            send_sem=xsend_sem.at[i], recv_sem=xrecv_sem.at[chip(i)],
            device_id=(sj, sp), device_id_type=MESH,
        ).wait_recv()
        acc = acc + xrecv[chip(i)]
    scale = 1.0 / (2.0 * nj)
    home = mine + x * block
    part[...] = acc * scale

    def spread(i):
        return pltpu.make_async_remote_copy(
            src_ref=part, dst_ref=cur1.at[pl.ds(home, block)],
            send_sem=gsend_sem.at[i], recv_sem=grecv_sem.at[x],
            device_id=(chip(i) * 2 + c, sp), device_id_type=MESH,
        )

    def spread_mate(src, where, n):
        return pltpu.make_async_remote_copy(
            src_ref=src, dst_ref=cur1.at[pl.ds(where, block)],
            send_sem=asend_sem.at[n], recv_sem=arecv_sem.at[n],
            device_id=(mate, sp), device_id_type=MESH,
        )

    for i in range(1, nx):
        spread(i).start()
    spread_mate(part, home, 0).start()
    cur1[pl.ds(home, block), :] = acc * scale
    for i in range(1, nx):
        where = mine + chip(i) * block
        pltpu.make_async_remote_copy(
            src_ref=part, dst_ref=cur1.at[pl.ds(where, block)],
            send_sem=gsend_sem.at[i], recv_sem=grecv_sem.at[chip(i)],
            device_id=(sj, sp), device_id_type=MESH,
        ).wait_recv()
        spread_mate(cur1.at[pl.ds(where, block)], where, i).start()
    for i in range(nx):
        where = other + chip(i) * block
        spread_mate(part, where, i).wait_recv()

    to_mate.wait_send()

    iterate(1)

    vel_out = pltpu.make_async_copy(f, out_h, out_sem.at[0])
    vel_out.start()

    for cc in range(2):
        for xx in range(nx):
            for p in range(pd):
                plane = (2 * xx + cc) * pd + p
                fsend[cc, xx, p] = total[pl.ds(plane, rows, stride=PLANE), :]
    planes_to_mate = pltpu.make_async_remote_copy(
        src_ref=fsend.at[1 - c], dst_ref=frecv,
        send_sem=fsend_sem.at[0], recv_sem=frecv_sem.at[0],
        device_id=(mate, sp), device_id_type=MESH,
    )
    planes_to_mate.start()
    planes_to_mate.wait_recv()
    fx[...] = fsend[c] + frecv[...]
    for i in range(1, nx):
        pltpu.make_async_remote_copy(
            src_ref=fx.at[chip(i)], dst_ref=fxrecv.at[x],
            send_sem=ysend_sem.at[i], recv_sem=yrecv_sem.at[x],
            device_id=(chip(i) * 2 + c, sp), device_id_type=MESH,
        ).start()
    acc = fx[x]
    for i in range(1, nx):
        pltpu.make_async_remote_copy(
            src_ref=fxrecv.at[0], dst_ref=fxrecv.at[chip(i)],
            send_sem=ysend_sem.at[i], recv_sem=yrecv_sem.at[chip(i)],
            device_id=(sj, sp), device_id_type=MESH,
        ).wait_recv()
        acc = acc + fxrecv[chip(i)]
    for p in range(pd):
        tout_ref[pl.ds(p, rows, stride=pd), :] = acc[p] * scale

    def sent_ask(j, carry):
        ask(j).wait_send()
        brick(0, j).wait_send()
        brick(1, j).wait_send()
        return carry

    lax.fori_loop(1, ns, sent_ask, 0)

    def sent_planes(i, carry):
        plane_copy(i).wait_send()
        return carry

    lax.fori_loop(1, nj, sent_planes, 0)
    for it in range(2):

        @pl.when(sp > 0)
        def _():
            edge_copy(it, 0).wait_send()

        @pl.when(sp < ns - 1)
        def _():
            edge_copy(it, 1).wait_send()

    planes_to_mate.wait_send()
    for i in range(nx):
        spread_mate(part, home, i).wait_send()
    for i in range(1, nx):
        spread(i).wait_send()
        pltpu.make_async_remote_copy(
            src_ref=xsend.at[pl.ds(chip(i) * block, block)], dst_ref=xrecv.at[x],
            send_sem=xsend_sem.at[i], recv_sem=xrecv_sem.at[x],
            device_id=(chip(i) * 2 + c, sp), device_id_type=MESH,
        ).wait_send()
        pltpu.make_async_remote_copy(
            src_ref=fx.at[chip(i)], dst_ref=fxrecv.at[x],
            send_sem=ysend_sem.at[i], recv_sem=yrecv_sem.at[x],
            device_id=(chip(i) * 2 + c, sp), device_id_type=MESH,
        ).wait_send()
    vel_out.wait()


def body(nj, ny, nz, images, velocity, weights, template, owners, local_rows, tile_counts):
    ns = ny * nz
    nx = nj // 2
    rows = images.shape[1]
    pd = template.shape[1]
    cap = 2 * rows // ns
    slots = ns * cap
    brick = (PLANE, LANES)
    piece = rows // nj * PLANE
    vmem = pl.BlockSpec(memory_space=pltpu.VMEM)
    smem = pl.BlockSpec(memory_space=pltpu.SMEM)
    away = pl.BlockSpec(memory_space=pl.ANY)
    bf16 = jnp.bfloat16
    dma = pltpu.SemaphoreType.DMA
    field, planes = pl.pallas_call(
        functools.partial(kernel, nj, ny, nz, rows, cap),
        out_shape=(
            jax.ShapeDtypeStruct(velocity.shape, F32),
            jax.ShapeDtypeStruct((rows * pd, LANES), F32),
        ),
        in_specs=[away, away, away, vmem, vmem, vmem, smem],
        out_specs=(away, vmem),
        scratch_shapes=[
            pltpu.VMEM((2, rows) + brick, bf16),
            pltpu.VMEM((3, 2, rows) + brick, bf16),
            pltpu.VMEM((3, 2, rows) + brick, F32),
            pltpu.VMEM((2, slots) + brick, bf16),
            pltpu.VMEM((slots,) + brick, bf16),
            pltpu.VMEM((slots,) + brick, bf16),
            pltpu.VMEM((2, rows) + brick, F32),
            pltpu.VMEM((3, 2, rows) + brick, F32),
            pltpu.VMEM((2, rows) + brick, F32),
            pltpu.VMEM((2, rows) + brick, F32),
            pltpu.VMEM((2, rows) + brick, F32),
            pltpu.VMEM((rows * PLANE, LANES), F32),
            pltpu.VMEM((rows * PLANE, LANES), F32),
            pltpu.VMEM((rows * PLANE, LANES), F32),
            pltpu.VMEM((pd, rows, LANES), F32),
            pltpu.VMEM((nj, pd, rows, LANES), F32),
            pltpu.VMEM((ns, 1, LANES), I32),
            pltpu.VMEM((ns, 1, LANES), I32),
            pltpu.VMEM((2, 1, LANES), I32),
            pltpu.SMEM((ns, 1, LANES), I32),
            pltpu.SMEM((2, 1, LANES), I32),
            pltpu.VMEM((2, 2, 3, 2) + brick, F32),
            pltpu.VMEM((2, 2, 3, 2) + brick, F32),
            pltpu.VMEM((piece, LANES), F32),
            pltpu.VMEM((rows // 2 * PLANE, LANES), F32),
            pltpu.VMEM((rows // 2 * PLANE, LANES), F32),
            pltpu.VMEM((nx, piece, LANES), F32),
            pltpu.VMEM((2, nx, pd, rows, LANES), F32),
            pltpu.VMEM((nx, pd, rows, LANES), F32),
            pltpu.VMEM((nx, pd, rows, LANES), F32),
            pltpu.VMEM((nx, pd, rows, LANES), F32),
            dma((3,)), dma((1,)), dma((nj,)), dma((nj,)), dma((ns,)), dma((ns,)), dma((3,)),
            dma((2, ns)), dma((2, ns)), dma((2, 2)), dma((2, 2)),
            dma((1,)), dma((1,)), dma((nx,)), dma((nx,)), dma((nx,)), dma((nx,)),
            dma((nx,)), dma((nx,)), dma((1,)), dma((1,)), dma((nx,)), dma((nx,)),
        ],
        compiler_params=pltpu.CompilerParams(
            collective_id=0, has_side_effects=True, vmem_limit_bytes=56 * 1024 * 1024
        ),
        name="demons",
    )(
        images, velocity, weights, template.reshape(rows * pd, LANES),
        jnp.swapaxes(owners, 1, 2), local_rows, tile_counts.T,
    )
    return field, planes.reshape(template.shape)


def solution(mesh):
    nj, ns = mesh.shape["subj"], mesh.shape["space"]
    nz = 8 if ns % 8 == 0 else 2
    in_specs = (
        P("subj", "space", None, None),
        P(None, "subj", "space", None, None),
        P(None, "subj", "space", None, None),
        P("space", "subj", None),
        P("subj", "space", None),
        P("subj", "space"),
        P("subj", "space"),
    )
    out_specs = (P(None, "subj", "space", None, None), P("space", "subj", None))
    return jax.shard_map(
        functools.partial(body, nj, ns // nz, nz),
        mesh=mesh, in_specs=in_specs, out_specs=out_specs, check_vma=False,
    )
```

```python
import functools

import jax
import jax.numpy as jnp
from jax import lax
from jax.experimental import pallas as pl
from jax.experimental.pallas import tpu as pltpu
from jax.sharding import PartitionSpec as P

MESH = pl.DeviceIdType.MESH
F32 = jnp.float32
I32 = jnp.int32
PLANE = 16
LANES = 128


def kernel(
    nj, ny, nz, rows, cap,
    img_h, vel_h, wts_h, tin_ref, own_ref, loc_ref, cnt_ref,
    f, tout_ref,
    img, wts, sendb, recvb0, recvb1, warp, g, q, r, pr, cur0, cur1, total,
    tsend, trecv, req, req_y, req_z, slot_v, rreq_s, slot_s, edge, halo,
    part, crecv, xsend, xrecv, fsend, frecv, fx, fxrecv,
    in_sem, tsend_sem, trecv_sem, qsend_sem, qrecv_sem, loc_sem,
    bsend_sem, brecv_sem, hsend_sem, hrecv_sem,
    csend_sem, crecv_sem, xsend_sem, xrecv_sem, gsend_sem, grecv_sem,
    asend_sem, arecv_sem, fsend_sem, frecv_sem, ysend_sem, yrecv_sem,
):
    ns = ny * nz
    nx = nj // 2
    pd = PLANE // nj
    sj = lax.axis_index("subj")
    sp = lax.axis_index("space")
    x, c = sj // 2, sj % 2
    y, z = sp // nz, sp % nz
    mate = x * 2 + (1 - c)
    recvb = (recvb0, recvb1)
    warp_step = 4
    step = max(2, rows // 8)
    half = rows // 2
    piece = rows // nj

    def peer(j):
        dy, zi = j % ny, j // ny
        dz = jnp.where(zi % 2 == 1, (zi + 1) // 2, nz - zi // 2)
        return ((y + dy) % ny) * nz + (z + dz) % nz

    img_in = pltpu.make_async_copy(img_h, img, in_sem.at[0])
    img_in.start()
    wts_in = pltpu.make_async_copy(wts_h, wts, in_sem.at[1])
    wts_in.start()
    vel_in = pltpu.make_async_copy(vel_h, f, in_sem.at[2])
    vel_in.start()

    barrier = pltpu.get_barrier_semaphore()

    def along_y(i):
        return ((y + i) % ny) * nz + z

    def along_z(i):
        return y * nz + (z + i) % nz

    for i in range(1, ny):
        pl.semaphore_signal(barrier, inc=1, device_id=(sj, along_y(i)), device_id_type=MESH)
    for i in range(1, nz):
        pl.semaphore_signal(barrier, inc=1, device_id=(sj, along_z(i)), device_id_type=MESH)

    def greet_subj(i, carry):
        pl.semaphore_signal(barrier, inc=1, device_id=((sj + i) % nj, sp), device_id_type=MESH)
        return carry

    lax.fori_loop(1, nj, greet_subj, 0)

    for p in range(pd):
        tsend[p] = tin_ref[pl.ds(p, rows, stride=pd), :]

    i0 = lax.broadcasted_iota(I32, (rows, rows), 0)
    i1 = lax.broadcasted_iota(I32, (rows, rows), 1)
    who = lax.broadcasted_iota(I32, (ns, rows), 0)
    lane = lax.broadcasted_iota(I32, (ns, LANES), 1)
    asked = jnp.zeros((ns, LANES), I32)
    slot_v[...] = jnp.zeros_like(slot_v)
    for s in range(2):
        count = cnt_ref[0, s]
        first = count // 2
        last = rows - (count - first)
        row = own_ref[s]
        col = jnp.sum(jnp.where(i0 == i1, row, 0), axis=1, keepdims=True)
        alive0 = (i0 < first) | (i0 >= last)
        hit = (col == row) & (i0 < i1) & alive0
        before = jnp.sum(jnp.where(hit, 1, 0), axis=0, keepdims=True)
        t1 = i1[0:1, :]
        alive1 = (t1 < first) | (t1 >= last)
        slot = jnp.where(alive1, row * cap + before, 0)
        slot_v[s, :, 0:rows] = slot
        place = jnp.where(alive1, before, cap)
        for k in range(cap):
            mine = (row == who) & (place == k)
            column = jnp.sum(jnp.where(mine, loc_ref[s : s + 1, :], 0), axis=1, keepdims=True)
            asked = asked + jnp.where(lane == s * cap + k, column, 0)
    for d in range(ns):
        req[d // nz, d % nz] = asked[d : d + 1, :]
    slots_in = pltpu.make_async_copy(slot_v, slot_s, loc_sem.at[0])
    slots_in.start()

    pl.semaphore_wait(barrier, ny - 1 + nz - 1 + nj - 1)

    def ask_y(i):
        return pltpu.make_async_remote_copy(
            src_ref=req.at[(y + i) % ny], dst_ref=req_y.at[y],
            send_sem=qsend_sem.at[0, i], recv_sem=qrecv_sem.at[0, y],
            device_id=(sj, along_y(i)), device_id_type=MESH,
        )

    def asked_y(i):
        return pltpu.make_async_remote_copy(
            src_ref=req.at[0], dst_ref=req_y.at[(y + i) % ny],
            send_sem=qsend_sem.at[0, i], recv_sem=qrecv_sem.at[0, (y + i) % ny],
            device_id=(sj, sp), device_id_type=MESH,
        )

    def ask_z(i):
        return pltpu.make_async_remote_copy(
            src_ref=req_y.at[:, (z + i) % nz], dst_ref=req_z.at[z],
            send_sem=qsend_sem.at[1, i], recv_sem=qrecv_sem.at[1, z],
            device_id=(sj, along_z(i)), device_id_type=MESH,
        )

    def asked_z(i):
        return pltpu.make_async_remote_copy(
            src_ref=req_y.at[:, 0], dst_ref=req_z.at[(z + i) % nz],
            send_sem=qsend_sem.at[1, i], recv_sem=qrecv_sem.at[1, (z + i) % nz],
            device_id=(sj, sp), device_id_type=MESH,
        )

    for i in range(1, ny):
        ask_y(i).start()
    req_y[y] = req[y]
    for i in range(1, ny):
        asked_y(i).wait_recv()
    for i in range(1, nz):
        ask_z(i).start()
    for n in range(ny):
        req_z[z, n] = req_y[n, z]

    def plane_copy(i):
        return pltpu.make_async_remote_copy(
            src_ref=tsend, dst_ref=trecv.at[sj],
            send_sem=tsend_sem.at[i], recv_sem=trecv_sem.at[sj],
            device_id=((sj + i) % nj, sp), device_id_type=MESH,
        )

    def start_planes(i, carry):
        plane_copy(i).start()
        return carry

    lax.fori_loop(1, nj, start_planes, 0)

    for i in range(1, nz):
        asked_z(i).wait_recv()
    rreq_in = pltpu.make_async_copy(req_z, rreq_s, loc_sem.at[2])
    rreq_in.start()
    img_in.wait()
    rreq_in.wait()

    def brick(s, j):
        d = peer(j)
        return pltpu.make_async_remote_copy(
            src_ref=sendb.at[s, pl.ds(d * cap, cap)], dst_ref=recvb[s].at[pl.ds(sp * cap, cap)],
            send_sem=bsend_sem.at[s, j], recv_sem=brecv_sem.at[s, sp],
            device_id=(sj, d), device_id_type=MESH,
        )

    def brick_from(s, d):
        return pltpu.make_async_remote_copy(
            src_ref=sendb.at[s, pl.ds(d * cap, cap)], dst_ref=recvb[s].at[pl.ds(d * cap, cap)],
            send_sem=bsend_sem.at[s, 0], recv_sem=brecv_sem.at[s, d],
            device_id=(sj, sp), device_id_type=MESH,
        )

    for s in range(2):

        def gather(j, carry):
            d = peer(j)
            for k in range(cap):
                sendb[s, d * cap + k] = img[s, rreq_s[d % nz, d // nz, 0, s * cap + k]]

            @pl.when(j >= 2)
            def _():
                brick(s, j - 1).start()

            return carry

        lax.fori_loop(1, ns, gather, 0)
        for k in range(cap):
            recvb[s][sp * cap + k] = img[s, rreq_s[z, y, 0, s * cap + k]]
        brick(s, ns - 1).start()

    def wait_planes(i, carry):
        other = (sj + i) % nj
        pltpu.make_async_remote_copy(
            src_ref=tsend, dst_ref=trecv.at[other],
            send_sem=tsend_sem.at[0], recv_sem=trecv_sem.at[other],
            device_id=(sj, sp), device_id_type=MESH,
        ).wait_recv()
        return carry

    lax.fori_loop(1, nj, wait_planes, 0)
    trecv[sj] = tsend[...]
    for j in range(nj):
        for p in range(pd):
            cur0[pl.ds(j * pd + p, rows, stride=PLANE), :] = trecv[j, p]

    @pl.when(sp == 0)
    def _():
        halo[:, 0] = jnp.zeros_like(halo[:, 0])

    @pl.when(sp == ns - 1)
    def _():
        halo[:, 1] = jnp.zeros_like(halo[:, 1])

    wts_in.wait()
    vel_in.wait()
    slots_in.wait()

    lanes = lax.broadcasted_iota(I32, (8, LANES), 1)
    subs = lax.broadcasted_iota(I32, (8, LANES), 0)
    low = subs < 4
    y_top = subs % 4 == 3
    y_bot = subs % 4 == 0
    z_top = lanes == LANES - 1
    z_bot = lanes == 0

    def up_z(v):
        return jnp.where(z_top, 0.0, pltpu.roll(v, LANES - 1, 1))

    def down_z(v):
        return jnp.where(z_bot, 0.0, pltpu.roll(v, 1, 1))

    def up_y(v):
        return jnp.where(y_top, 0.0, pltpu.roll(v, 7, 0))

    def down_y(v):
        return jnp.where(y_bot, 0.0, pltpu.roll(v, 1, 0))

    def up_x(pair):
        a, b = [pltpu.roll(v, 4, 0) for v in pair]
        return [jnp.where(low, a, b), jnp.where(low, b, 0.0)]

    def pair_of(value):
        return [value[0:8], value[8:16]]

    def put(ref, index, pair):
        ref[index + (slice(0, 8),)] = pair[0]
        ref[index + (slice(8, 16),)] = pair[1]

    both = (0, 1)

    for s in range(2):

        def arrived(j, carry):
            brick_from(s, peer(j)).wait_recv()
            return carry

        lax.fori_loop(1, ns, arrived, 0)
        count = cnt_ref[0, s]
        first = count // 2
        last = rows - (count - first)

        def warp_tile(t):
            b00 = pair_of(recvb[s][slot_s[s, 0, t]].astype(F32))
            wx, wy, wz = [pair_of(wts[a, s, t].astype(F32)) for a in range(3)]
            live = jnp.where((t < first) | (t >= last), 1.0, 0.0).astype(F32)
            d00 = [up_z(v) - v for v in b00]
            b01, d01 = [up_y(v) for v in b00], [up_y(v) for v in d00]
            b10, d10 = up_x(b00), up_x(d00)
            b11, d11 = up_x(b01), up_x(d01)
            w = []
            for i in both:
                l00 = b00[i] + wz[i] * d00[i]
                l01 = b01[i] + wz[i] * d01[i]
                l10 = b10[i] + wz[i] * d10[i]
                l11 = b11[i] + wz[i] * d11[i]
                m0 = l00 + wy[i] * (l01 - l00)
                m1 = l10 + wy[i] * (l11 - l10)
                w.append((m0 + wx[i] * (m1 - m0)) * live)
            h = [0.5 * v for v in w]
            ra, rb = [pltpu.roll(v, 4, 0) for v in h]
            mid = jnp.where(low, ra, rb)
            gx = [mid - jnp.where(low, 0.0, ra), jnp.where(low, rb, 0.0) - mid]
            gy = [up_y(v) - down_y(v) for v in h]
            gz = [up_z(v) - down_z(v) for v in h]
            here = pl.multiple_of(t * PLANE, PLANE)
            now = pair_of(cur0[pl.ds(here, PLANE), :])
            fx0, fy0, fz0 = [pair_of(f[a, s, t]) for a in range(3)]
            qq, rr = [], []
            for i in both:
                sq = gx[i] * gx[i] + gy[i] * gy[i] + gz[i] * gz[i]
                inverse = 1.0 / (16.0 * sq + 4.0)
                pred = w[i] + (gx[i] * fx0[i] + gy[i] * fy0[i]) + gz[i] * fz0[i]
                qq.append(inverse)
                rr.append((pred - now[i]) * inverse)
            put(warp, (s, t), w)
            put(g, (0, s, t), gx)
            put(g, (1, s, t), gy)
            put(g, (2, s, t), gz)
            put(q, (s, t), qq)
            put(r, (s, t), rr)

        def warp_block(b, carry):
            for n in range(warp_step):
                warp_tile(b * warp_step + n)
            return carry

        lax.fori_loop(0, rows // warp_step, warp_block, 0)

    def first_ratio(s, t):
        return pair_of(r[s, t])

    def second_ratio(s, t):
        here = pl.multiple_of(t * PLANE, PLANE)
        now = pair_of(cur1[pl.ds(here, PLANE), :])
        p1 = pair_of(pr[s, t])
        qq = pair_of(q[s, t])
        return [(p1[i] - now[i]) * qq[i] for i in both]

    def edge_copy(it, side):
        d = sp - 1 if side == 0 else sp + 1
        return pltpu.make_async_remote_copy(
            src_ref=edge.at[it, side], dst_ref=halo.at[it, 1 - side],
            send_sem=hsend_sem.at[it, side], recv_sem=hrecv_sem.at[it, 1 - side],
            device_id=(sj, d), device_id_type=MESH,
        )

    def halo_in(it, side):
        return pltpu.make_async_remote_copy(
            src_ref=edge.at[it, side], dst_ref=halo.at[it, side],
            send_sem=hsend_sem.at[it, side], recv_sem=hrecv_sem.at[it, side],
            device_id=(sj, sp), device_id_type=MESH,
        )

    def iterate(it):
        ratio = first_ratio if it == 0 else second_ratio

        def update(s, t):
            rr = ratio(s, t)
            out = []
            for a in range(3):
                gg = pair_of(g[a, s, t])
                out += [gg[0] * rr[0], gg[1] * rr[1]]
            return out

        for s in range(2):
            for side, t in ((0, 0), (1, rows - 1)):
                u = update(s, t)
                for a in range(3):
                    put(edge, (it, side, a, s), u[2 * a : 2 * a + 2])

        @pl.when(sp > 0)
        def _():
            edge_copy(it, 0).start()

        @pl.when(sp < ns - 1)
        def _():
            edge_copy(it, 1).start()

        def advance(s, t, v):
            new = []
            for a in range(3):
                old = pair_of(f[a, s, t])
                out = []
                for i in both:
                    value = v[2 * a + i]
                    two = value + down_z(value)
                    out.append(old[i] - (two + jnp.where(z_top, value, pltpu.roll(two, LANES - 1, 1))))
                put(f, (a, s, t), out)
                new.append(out)
            w = pair_of(warp[s, t])
            gg = [pair_of(g[a, s, t]) for a in range(3)]
            pred = [
                w[i] + (gg[0][i] * new[0][i] + gg[1][i] * new[1][i]) + gg[2][i] * new[2][i]
                for i in both
            ]
            if it == 0:
                put(pr, (s, t), pred)
            here = pl.multiple_of(t * PLANE, PLANE)
            if s == 0:
                total[pl.ds(here, 8), :] = pred[0]
                total[pl.ds(here + 8, 8), :] = pred[1]
            else:
                total[pl.ds(here, 8), :] = total[pl.ds(here, 8), :] + pred[0]
                total[pl.ds(here + 8, 8), :] = total[pl.ds(here + 8, 8), :] + pred[1]

        def add(p, o):
            return [a + b for a, b in zip(p, o)]

        def run(s, start, low_row, high_row):
            u = update(s, start)
            two = add(low_row or update(s, start - 1), u)
            for n in range(step):
                at_end = n == step - 1
                after = high_row if at_end and high_row else update(s, start + n + 1)
                ahead = add(u, after)
                advance(s, start + n, add(two, ahead))
                u, two = after, ahead

        for s in range(2):

            def inner(b, carry):
                run(s, b * step, None, None)
                return carry

            lax.fori_loop(1, rows // step - 1, inner, 0)

        @pl.when(sp > 0)
        def _():
            halo_in(it, 0).wait_recv()

        @pl.when(sp < ns - 1)
        def _():
            halo_in(it, 1).wait_recv()

        def halo_row(side, s):
            out = []
            for a in range(3):
                out += pair_of(halo[it, side, a, s])
            return out

        for s in range(2):
            run(s, 0, halo_row(0, s), None)
            run(s, rows - step, None, halo_row(1, s))

    iterate(0)

    mine = c * half * PLANE
    other = (1 - c) * half * PLANE
    span = half * PLANE
    block = piece * PLANE

    to_mate = pltpu.make_async_remote_copy(
        src_ref=total.at[pl.ds(other, span)], dst_ref=crecv,
        send_sem=csend_sem.at[0], recv_sem=crecv_sem.at[0],
        device_id=(mate, sp), device_id_type=MESH,
    )
    to_mate.start()
    to_mate.wait_recv()
    xsend[...] = total[pl.ds(mine, span), :] + crecv[...]

    def chip(i):
        return (x + i) % nx

    for i in range(1, nx):
        pltpu.make_async_remote_copy(
            src_ref=xsend.at[pl.ds(chip(i) * block, block)], dst_ref=xrecv.at[x],
            send_sem=xsend_sem.at[i], recv_sem=xrecv_sem.at[x],
            device_id=(chip(i) * 2 + c, sp), device_id_type=MESH,
        ).start()
    acc = xsend[pl.ds(x * block, block), :]
    for i in range(1, nx):
        pltpu.make_async_remote_copy(
            src_ref=xrecv.at[0], dst_ref=xrecv.at[chip(i)],
            send_sem=xsend_sem.at[i], recv_sem=xrecv_sem.at[chip(i)],
            device_id=(sj, sp), device_id_type=MESH,
        ).wait_recv()
        acc = acc + xrecv[chip(i)]
    scale = 1.0 / (2.0 * nj)
    home = mine + x * block
    part[...] = acc * scale

    def spread(i):
        return pltpu.make_async_remote_copy(
            src_ref=part, dst_ref=cur1.at[pl.ds(home, block)],
            send_sem=gsend_sem.at[i], recv_sem=grecv_sem.at[x],
            device_id=(chip(i) * 2 + c, sp), device_id_type=MESH,
        )

    def spread_mate(src, where, n):
        return pltpu.make_async_remote_copy(
            src_ref=src, dst_ref=cur1.at[pl.ds(where, block)],
            send_sem=asend_sem.at[n], recv_sem=arecv_sem.at[n],
            device_id=(mate, sp), device_id_type=MESH,
        )

    for i in range(1, nx):
        spread(i).start()
    spread_mate(part, home, 0).start()
    cur1[pl.ds(home, block), :] = acc * scale
    for i in range(1, nx):
        where = mine + chip(i) * block
        pltpu.make_async_remote_copy(
            src_ref=part, dst_ref=cur1.at[pl.ds(where, block)],
            send_sem=gsend_sem.at[i], recv_sem=grecv_sem.at[chip(i)],
            device_id=(sj, sp), device_id_type=MESH,
        ).wait_recv()
        spread_mate(cur1.at[pl.ds(where, block)], where, i).start()
    for i in range(nx):
        where = other + chip(i) * block
        spread_mate(part, where, i).wait_recv()

    to_mate.wait_send()

    iterate(1)

    for cc in range(2):
        for xx in range(nx):
            for p in range(pd):
                plane = (2 * xx + cc) * pd + p
                fsend[cc, xx, p] = total[pl.ds(plane, rows, stride=PLANE), :]
    planes_to_mate = pltpu.make_async_remote_copy(
        src_ref=fsend.at[1 - c], dst_ref=frecv,
        send_sem=fsend_sem.at[0], recv_sem=frecv_sem.at[0],
        device_id=(mate, sp), device_id_type=MESH,
    )
    planes_to_mate.start()
    planes_to_mate.wait_recv()
    fx[...] = fsend[c] + frecv[...]
    for i in range(1, nx):
        pltpu.make_async_remote_copy(
            src_ref=fx.at[chip(i)], dst_ref=fxrecv.at[x],
            send_sem=ysend_sem.at[i], recv_sem=yrecv_sem.at[x],
            device_id=(chip(i) * 2 + c, sp), device_id_type=MESH,
        ).start()
    acc = fx[x]
    for i in range(1, nx):
        pltpu.make_async_remote_copy(
            src_ref=fxrecv.at[0], dst_ref=fxrecv.at[chip(i)],
            send_sem=ysend_sem.at[i], recv_sem=yrecv_sem.at[chip(i)],
            device_id=(sj, sp), device_id_type=MESH,
        ).wait_recv()
        acc = acc + fxrecv[chip(i)]
    for p in range(pd):
        tout_ref[pl.ds(p, rows, stride=pd), :] = acc[p] * scale

    for i in range(1, ny):
        ask_y(i).wait_send()
    for i in range(1, nz):
        ask_z(i).wait_send()

    def sent_bricks(j, carry):
        brick(0, j).wait_send()
        brick(1, j).wait_send()
        return carry

    lax.fori_loop(1, ns, sent_bricks, 0)

    def sent_planes(i, carry):
        plane_copy(i).wait_send()
        return carry

    lax.fori_loop(1, nj, sent_planes, 0)
    for it in range(2):

        @pl.when(sp > 0)
        def _():
            edge_copy(it, 0).wait_send()

        @pl.when(sp < ns - 1)
        def _():
            edge_copy(it, 1).wait_send()

    planes_to_mate.wait_send()
    for i in range(nx):
        spread_mate(part, home, i).wait_send()
    for i in range(1, nx):
        spread(i).wait_send()
        pltpu.make_async_remote_copy(
            src_ref=xsend.at[pl.ds(chip(i) * block, block)], dst_ref=xrecv.at[x],
            send_sem=xsend_sem.at[i], recv_sem=xrecv_sem.at[x],
            device_id=(chip(i) * 2 + c, sp), device_id_type=MESH,
        ).wait_send()
        pltpu.make_async_remote_copy(
            src_ref=fx.at[chip(i)], dst_ref=fxrecv.at[x],
            send_sem=ysend_sem.at[i], recv_sem=yrecv_sem.at[x],
            device_id=(chip(i) * 2 + c, sp), device_id_type=MESH,
        ).wait_send()


def body(nj, ny, nz, images, velocity, weights, template, owners, local_rows, tile_counts):
    ns = ny * nz
    nx = nj // 2
    rows = images.shape[1]
    pd = template.shape[1]
    cap = 2 * rows // ns
    slots = ns * cap
    brick = (PLANE, LANES)
    piece = rows // nj * PLANE
    vmem = pl.BlockSpec(memory_space=pltpu.VMEM)
    smem = pl.BlockSpec(memory_space=pltpu.SMEM)
    away = pl.BlockSpec(memory_space=pltpu.HBM)
    bf16 = jnp.bfloat16
    dma = pltpu.SemaphoreType.DMA
    field, planes = pl.pallas_call(
        functools.partial(kernel, nj, ny, nz, rows, cap),
        out_shape=(
            pltpu.VMEM(velocity.shape, F32),
            jax.ShapeDtypeStruct((rows * pd, LANES), F32),
        ),
        in_specs=[away, away, away, vmem, vmem, vmem, smem],
        out_specs=(vmem, vmem),
        scratch_shapes=[
            pltpu.VMEM((2, rows) + brick, bf16),
            pltpu.VMEM((3, 2, rows) + brick, bf16),
            pltpu.VMEM((2, slots) + brick, bf16),
            pltpu.VMEM((slots,) + brick, bf16),
            pltpu.VMEM((slots,) + brick, bf16),
            pltpu.VMEM((2, rows) + brick, F32),
            pltpu.VMEM((3, 2, rows) + brick, F32),
            pltpu.VMEM((2, rows) + brick, F32),
            pltpu.VMEM((2, rows) + brick, F32),
            pltpu.VMEM((2, rows) + brick, F32),
            pltpu.VMEM((rows * PLANE, LANES), F32),
            pltpu.VMEM((rows * PLANE, LANES), F32),
            pltpu.VMEM((rows * PLANE, LANES), F32),
            pltpu.VMEM((pd, rows, LANES), F32),
            pltpu.VMEM((nj, pd, rows, LANES), F32),
            pltpu.VMEM((ny, nz, 1, LANES), I32),
            pltpu.VMEM((ny, nz, 1, LANES), I32),
            pltpu.VMEM((nz, ny, 1, LANES), I32),
            pltpu.VMEM((2, 1, LANES), I32),
            pltpu.SMEM((nz, ny, 1, LANES), I32),
            pltpu.SMEM((2, 1, LANES), I32),
            pltpu.VMEM((2, 2, 3, 2) + brick, F32),
            pltpu.VMEM((2, 2, 3, 2) + brick, F32),
            pltpu.VMEM((piece, LANES), F32),
            pltpu.VMEM((rows // 2 * PLANE, LANES), F32),
            pltpu.VMEM((rows // 2 * PLANE, LANES), F32),
            pltpu.VMEM((nx, piece, LANES), F32),
            pltpu.VMEM((2, nx, pd, rows, LANES), F32),
            pltpu.VMEM((nx, pd, rows, LANES), F32),
            pltpu.VMEM((nx, pd, rows, LANES), F32),
            pltpu.VMEM((nx, pd, rows, LANES), F32),
            dma((3,)), dma((nj,)), dma((nj,)), dma((2, nz)), dma((2, nz)), dma((4,)),
            dma((2, ns)), dma((2, ns)), dma((2, 2)), dma((2, 2)),
            dma((1,)), dma((1,)), dma((nx,)), dma((nx,)), dma((nx,)), dma((nx,)),
            dma((nx,)), dma((nx,)), dma((1,)), dma((1,)), dma((nx,)), dma((nx,)),
        ],
        compiler_params=pltpu.CompilerParams(
            collective_id=0, has_side_effects=True, vmem_limit_bytes=62200 * 1024
        ),
        name="demons",
    )(
        images, velocity, weights, template.reshape(rows * pd, LANES),
        jnp.swapaxes(owners, 1, 2), local_rows, tile_counts.T,
    )
    return field, planes.reshape(template.shape)


def solution(mesh):
    nj, ns = mesh.shape["subj"], mesh.shape["space"]
    nz = 8 if ns % 8 == 0 else 2
    in_specs = (
        P("subj", "space", None, None),
        P(None, "subj", "space", None, None),
        P(None, "subj", "space", None, None),
        P("space", "subj", None),
        P("subj", "space", None),
        P("subj", "space"),
        P("subj", "space"),
    )
    out_specs = (P(None, "subj", "space", None, None), P("space", "subj", None))
    return jax.shard_map(
        functools.partial(body, nj, ns // nz, nz),
        mesh=mesh, in_specs=in_specs, out_specs=out_specs, check_vma=False,
    )
```

```python
import functools

import jax
import jax.numpy as jnp
from jax import lax
from jax.experimental import pallas as pl
from jax.experimental.pallas import tpu as pltpu
from jax.sharding import PartitionSpec as P

MESH = pl.DeviceIdType.MESH
F32 = jnp.float32
I32 = jnp.int32
PLANE = 16
LANES = 128


def kernel(
    nj, ny, nz, rows, cap,
    img_h, vel_h, wts_h, tin_ref, own_ref, loc_ref, cnt_ref,
    f, tout_ref,
    img, wts, sendb, recvb0, recvb1, warp, g, q, r, pr, cur0, cur1, total,
    tsend, trecv, req, req_y, req_z, slot_v, rreq_s, slot_s, edge, halo,
    part, crecv, xsend, xrecv, fsend, frecv, fx, fxrecv,
    in_sem, tsend_sem, trecv_sem, qsend_sem, qrecv_sem, loc_sem,
    bsend_sem, brecv_sem, hsend_sem, hrecv_sem,
    csend_sem, crecv_sem, xsend_sem, xrecv_sem, gsend_sem, grecv_sem,
    asend_sem, arecv_sem, fsend_sem, frecv_sem, ysend_sem, yrecv_sem,
):
    ns = ny * nz
    nx = nj // 2
    pd = PLANE // nj
    sj = lax.axis_index("subj")
    sp = lax.axis_index("space")
    x, c = sj // 2, sj % 2
    y, z = sp // nz, sp % nz
    mate = x * 2 + (1 - c)
    recvb = (recvb0, recvb1)
    warp_step = 4 if rows >= 32 else 2
    step = max(2, rows // 8)

    def peer(j):
        dy, zi = j % ny, j // ny
        dz = jnp.where(zi % 2 == 1, (zi + 1) // 2, nz - zi // 2)
        return ((y + dy) % ny) * nz + (z + dz) % nz

    img_in = pltpu.make_async_copy(img_h, img, in_sem.at[0])
    img_in.start()
    wts_in = pltpu.make_async_copy(wts_h, wts, in_sem.at[1])
    wts_in.start()
    vel_in = pltpu.make_async_copy(vel_h, f, in_sem.at[2])
    vel_in.start()

    barrier = pltpu.get_barrier_semaphore()

    def along_y(i):
        return ((y + i) % ny) * nz + z

    def along_z(i):
        return y * nz + (z + i) % nz

    for i in range(1, ny):
        pl.semaphore_signal(barrier, inc=1, device_id=(sj, along_y(i)), device_id_type=MESH)
    for i in range(1, nz):
        pl.semaphore_signal(barrier, inc=1, device_id=(sj, along_z(i)), device_id_type=MESH)

    def greet_subj(i, carry):
        pl.semaphore_signal(barrier, inc=1, device_id=((sj + i) % nj, sp), device_id_type=MESH)
        return carry

    lax.fori_loop(1, nj, greet_subj, 0)

    for p in range(pd):
        tsend[p] = tin_ref[pl.ds(p, rows, stride=pd), :]

    i0 = lax.broadcasted_iota(I32, (rows, rows), 0)
    i1 = lax.broadcasted_iota(I32, (rows, rows), 1)
    who = lax.broadcasted_iota(I32, (ns, rows), 0)
    lane = lax.broadcasted_iota(I32, (ns, LANES), 1)
    asked = jnp.zeros((ns, LANES), I32)
    slot_v[...] = jnp.zeros_like(slot_v)
    for s in range(2):
        count = cnt_ref[0, s]
        first = count // 2
        last = rows - (count - first)
        row = own_ref[s]
        col = jnp.sum(jnp.where(i0 == i1, row, 0), axis=1, keepdims=True)
        alive0 = (i0 < first) | (i0 >= last)
        hit = (col == row) & (i0 < i1) & alive0
        before = jnp.sum(jnp.where(hit, 1, 0), axis=0, keepdims=True)
        t1 = i1[0:1, :]
        alive1 = (t1 < first) | (t1 >= last)
        slot = jnp.where(alive1, row * cap + before, 0)
        slot_v[s, :, 0:rows] = slot
        place = jnp.where(alive1, before, cap)
        for k in range(cap):
            mine = (row == who) & (place == k)
            column = jnp.sum(jnp.where(mine, loc_ref[s : s + 1, :], 0), axis=1, keepdims=True)
            asked = asked + jnp.where(lane == s * cap + k, column, 0)
    for d in range(ns):
        req[d // nz, d % nz] = asked[d : d + 1, :]
    slots_in = pltpu.make_async_copy(slot_v, slot_s, loc_sem.at[0])
    slots_in.start()

    pl.semaphore_wait(barrier, ny - 1 + nz - 1 + nj - 1)

    def ask_y(i):
        return pltpu.make_async_remote_copy(
            src_ref=req.at[(y + i) % ny], dst_ref=req_y.at[y],
            send_sem=qsend_sem.at[0, i], recv_sem=qrecv_sem.at[0, y],
            device_id=(sj, along_y(i)), device_id_type=MESH,
        )

    def asked_y(i):
        return pltpu.make_async_remote_copy(
            src_ref=req.at[0], dst_ref=req_y.at[(y + i) % ny],
            send_sem=qsend_sem.at[0, i], recv_sem=qrecv_sem.at[0, (y + i) % ny],
            device_id=(sj, sp), device_id_type=MESH,
        )

    def ask_z(i):
        return pltpu.make_async_remote_copy(
            src_ref=req_y.at[:, (z + i) % nz], dst_ref=req_z.at[z],
            send_sem=qsend_sem.at[1, i], recv_sem=qrecv_sem.at[1, z],
            device_id=(sj, along_z(i)), device_id_type=MESH,
        )

    def asked_z(i):
        return pltpu.make_async_remote_copy(
            src_ref=req_y.at[:, 0], dst_ref=req_z.at[(z + i) % nz],
            send_sem=qsend_sem.at[1, i], recv_sem=qrecv_sem.at[1, (z + i) % nz],
            device_id=(sj, sp), device_id_type=MESH,
        )

    for i in range(1, ny):
        ask_y(i).start()
    req_y[y] = req[y]
    for i in range(1, ny):
        asked_y(i).wait_recv()
    for i in range(1, nz):
        ask_z(i).start()
    for n in range(ny):
        req_z[z, n] = req_y[n, z]

    def plane_copy(i):
        return pltpu.make_async_remote_copy(
            src_ref=tsend, dst_ref=trecv.at[sj],
            send_sem=tsend_sem.at[i], recv_sem=trecv_sem.at[sj],
            device_id=((sj + i) % nj, sp), device_id_type=MESH,
        )

    def start_planes(i, carry):
        plane_copy(i).start()
        return carry

    lax.fori_loop(1, nj, start_planes, 0)

    for i in range(1, nz):
        asked_z(i).wait_recv()
    rreq_in = pltpu.make_async_copy(req_z, rreq_s, loc_sem.at[2])
    rreq_in.start()
    img_in.wait()
    rreq_in.wait()

    def brick(s, j):
        d = peer(j)
        return pltpu.make_async_remote_copy(
            src_ref=sendb.at[s, pl.ds(d * cap, cap)], dst_ref=recvb[s].at[pl.ds(sp * cap, cap)],
            send_sem=bsend_sem.at[s, j], recv_sem=brecv_sem.at[s, sp],
            device_id=(sj, d), device_id_type=MESH,
        )

    def brick_from(s, d):
        return pltpu.make_async_remote_copy(
            src_ref=sendb.at[s, pl.ds(d * cap, cap)], dst_ref=recvb[s].at[pl.ds(d * cap, cap)],
            send_sem=bsend_sem.at[s, 0], recv_sem=brecv_sem.at[s, d],
            device_id=(sj, sp), device_id_type=MESH,
        )

    for s in range(2):

        def gather(j, carry):
            d = peer(j)
            for k in range(cap):
                sendb[s, d * cap + k] = img[s, rreq_s[d % nz, d // nz, 0, s * cap + k]]

            @pl.when(j >= 2)
            def _():
                brick(s, j - 1).start()

            return carry

        lax.fori_loop(1, ns, gather, 0)
        for k in range(cap):
            recvb[s][sp * cap + k] = img[s, rreq_s[z, y, 0, s * cap + k]]
        brick(s, ns - 1).start()

    def wait_planes(i, carry):
        other = (sj + i) % nj
        pltpu.make_async_remote_copy(
            src_ref=tsend, dst_ref=trecv.at[other],
            send_sem=tsend_sem.at[0], recv_sem=trecv_sem.at[other],
            device_id=(sj, sp), device_id_type=MESH,
        ).wait_recv()
        return carry

    lax.fori_loop(1, nj, wait_planes, 0)
    trecv[sj] = tsend[...]
    for j in range(nj):
        for p in range(pd):
            cur0[pl.ds(j * pd + p, rows, stride=PLANE), :] = trecv[j, p]

    @pl.when(sp == 0)
    def _():
        halo[:, 0] = jnp.zeros_like(halo[:, 0])

    @pl.when(sp == ns - 1)
    def _():
        halo[:, 1] = jnp.zeros_like(halo[:, 1])

    wts_in.wait()
    vel_in.wait()
    slots_in.wait()

    lanes = lax.broadcasted_iota(I32, (8, LANES), 1)
    subs = lax.broadcasted_iota(I32, (8, LANES), 0)
    low = subs < 4
    y_top = subs % 4 == 3
    y_bot = subs % 4 == 0
    z_top = lanes == LANES - 1
    z_bot = lanes == 0

    def up_z(v):
        return jnp.where(z_top, 0.0, pltpu.roll(v, LANES - 1, 1))

    def down_z(v):
        return jnp.where(z_bot, 0.0, pltpu.roll(v, 1, 1))

    def up_y(v):
        return jnp.where(y_top, 0.0, pltpu.roll(v, 7, 0))

    def down_y(v):
        return jnp.where(y_bot, 0.0, pltpu.roll(v, 1, 0))

    def up_x(pair):
        a, b = [pltpu.roll(v, 4, 0) for v in pair]
        return [jnp.where(low, a, b), jnp.where(low, b, 0.0)]

    def pair_of(value):
        return [value[0:8], value[8:16]]

    def put(ref, index, pair):
        ref[index + (slice(0, 8),)] = pair[0]
        ref[index + (slice(8, 16),)] = pair[1]

    both = (0, 1)

    def arrivals(s):
        def arrived(j, carry):
            brick_from(s, peer(j)).wait_recv()
            return carry

        lax.fori_loop(1, ns, arrived, 0)

    def warp_blocks(s, start, stop):
        count = cnt_ref[0, s]
        first = count // 2
        last = rows - (count - first)

        def warp_tile(t):
            b00 = pair_of(recvb[s][slot_s[s, 0, t]].astype(F32))
            wx, wy, wz = [pair_of(wts[a, s, t].astype(F32)) for a in range(3)]
            live = jnp.where((t < first) | (t >= last), 1.0, 0.0).astype(F32)
            d00 = [up_z(v) - v for v in b00]
            b01, d01 = [up_y(v) for v in b00], [up_y(v) for v in d00]
            b10, d10 = up_x(b00), up_x(d00)
            b11, d11 = up_x(b01), up_x(d01)
            w = []
            for i in both:
                l00 = b00[i] + wz[i] * d00[i]
                l01 = b01[i] + wz[i] * d01[i]
                l10 = b10[i] + wz[i] * d10[i]
                l11 = b11[i] + wz[i] * d11[i]
                m0 = l00 + wy[i] * (l01 - l00)
                m1 = l10 + wy[i] * (l11 - l10)
                w.append((m0 + wx[i] * (m1 - m0)) * live)
            h = [0.5 * v for v in w]
            ra, rb = [pltpu.roll(v, 4, 0) for v in h]
            mid = jnp.where(low, ra, rb)
            gx = [mid - jnp.where(low, 0.0, ra), jnp.where(low, rb, 0.0) - mid]
            gy = [up_y(v) - down_y(v) for v in h]
            gz = [up_z(v) - down_z(v) for v in h]
            here = pl.multiple_of(t * PLANE, PLANE)
            now = pair_of(cur0[pl.ds(here, PLANE), :])
            fx0, fy0, fz0 = [pair_of(f[a, s, t]) for a in range(3)]
            qq, rr = [], []
            for i in both:
                sq = gx[i] * gx[i] + gy[i] * gy[i] + gz[i] * gz[i]
                inverse = 1.0 / (16.0 * sq + 4.0)
                pred = w[i] + (gx[i] * fx0[i] + gy[i] * fy0[i]) + gz[i] * fz0[i]
                qq.append(inverse)
                rr.append((pred - now[i]) * inverse)
            put(warp, (s, t), w)
            put(g, (0, s, t), gx)
            put(g, (1, s, t), gy)
            put(g, (2, s, t), gz)
            put(q, (s, t), qq)
            put(r, (s, t), rr)

        def warp_block(b, carry):
            for n in range(warp_step):
                warp_tile(b * warp_step + n)
            return carry

        lax.fori_loop(start, stop, warp_block, 0)

    def first_ratio(s, t):
        return pair_of(r[s, t])

    def second_ratio(s, t):
        here = pl.multiple_of(t * PLANE, PLANE)
        now = pair_of(cur1[pl.ds(here, PLANE), :])
        p1 = pair_of(pr[s, t])
        qq = pair_of(q[s, t])
        return [(p1[i] - now[i]) * qq[i] for i in both]

    def edge_copy(it, side, s):
        d = sp - 1 if side == 0 else sp + 1
        return pltpu.make_async_remote_copy(
            src_ref=edge.at[it, side, s], dst_ref=halo.at[it, 1 - side, s],
            send_sem=hsend_sem.at[it, side, s], recv_sem=hrecv_sem.at[it, 1 - side, s],
            device_id=(sj, d), device_id_type=MESH,
        )

    def halo_in(it, side, s):
        return pltpu.make_async_remote_copy(
            src_ref=edge.at[it, side, s], dst_ref=halo.at[it, side, s],
            send_sem=hsend_sem.at[it, side, s], recv_sem=hrecv_sem.at[it, side, s],
            device_id=(sj, sp), device_id_type=MESH,
        )

    def inside(side):
        return sp > 0 if side == 0 else sp < ns - 1

    def update(it, s, t):
        rr = first_ratio(s, t) if it == 0 else second_ratio(s, t)
        out = []
        for a in range(3):
            gg = pair_of(g[a, s, t])
            out += [gg[0] * rr[0], gg[1] * rr[1]]
        return out

    def send_edge(it, side, s):
        u = update(it, s, 0 if side == 0 else rows - 1)
        for a in range(3):
            put(edge, (it, side, s, a), u[2 * a : 2 * a + 2])

        @pl.when(inside(side))
        def _():
            edge_copy(it, side, s).start()

    def wait_halo(it, side, s):
        @pl.when(inside(side))
        def _():
            halo_in(it, side, s).wait_recv()

    def advance(it, s, t, v):
        new = []
        for a in range(3):
            old = pair_of(f[a, s, t])
            out = []
            for i in both:
                value = v[2 * a + i]
                two = value + down_z(value)
                out.append(old[i] - (two + jnp.where(z_top, value, pltpu.roll(two, LANES - 1, 1))))
            put(f, (a, s, t), out)
            new.append(out)
        w = pair_of(warp[s, t])
        gg = [pair_of(g[a, s, t]) for a in range(3)]
        pred = [
            w[i] + (gg[0][i] * new[0][i] + gg[1][i] * new[1][i]) + gg[2][i] * new[2][i]
            for i in both
        ]
        if it == 0:
            put(pr, (s, t), pred)
        here = pl.multiple_of(t * PLANE, PLANE)
        if s == 0:
            total[pl.ds(here, 8), :] = pred[0]
            total[pl.ds(here + 8, 8), :] = pred[1]
        else:
            total[pl.ds(here, 8), :] = total[pl.ds(here, 8), :] + pred[0]
            total[pl.ds(here + 8, 8), :] = total[pl.ds(here + 8, 8), :] + pred[1]

    def add(p, o):
        return [a + b for a, b in zip(p, o)]

    def run(it, s, start, low_row, high_row):
        u = update(it, s, start)
        two = add(low_row or update(it, s, start - 1), u)
        for n in range(step):
            at_end = n == step - 1
            after = high_row if at_end and high_row else update(it, s, start + n + 1)
            ahead = add(u, after)
            advance(it, s, start + n, add(two, ahead))
            u, two = after, ahead

    def smooth(it, s, start, stop):
        def inner(b, carry):
            run(it, s, b * step, None, None)
            return carry

        lax.fori_loop(start, stop, inner, 0)

    def smooth_edge(it, side, s):
        far = []
        for a in range(3):
            far += pair_of(halo[it, side, s, a])
        if side == 0:
            run(it, s, 0, far, None)
        else:
            run(it, s, rows - step, None, far)

    def chip(i):
        return (x + i) % nx

    quarter = rows // 4 * PLANE
    block = rows // (2 * nj) * PLANE
    scale = 1.0 / (2.0 * nj)

    def mine(k):
        return (2 * k + c) * quarter

    def other(k):
        return (2 * k + 1 - c) * quarter

    def to_mate(k):
        return pltpu.make_async_remote_copy(
            src_ref=total.at[pl.ds(other(k), quarter)], dst_ref=crecv.at[k],
            send_sem=csend_sem.at[k], recv_sem=crecv_sem.at[k],
            device_id=(mate, sp), device_id_type=MESH,
        )

    def across(k, i):
        return pltpu.make_async_remote_copy(
            src_ref=xsend.at[k, pl.ds(chip(i) * block, block)], dst_ref=xrecv.at[k, x],
            send_sem=xsend_sem.at[k, i], recv_sem=xrecv_sem.at[k, x],
            device_id=(chip(i) * 2 + c, sp), device_id_type=MESH,
        )

    def spread(k, i):
        return pltpu.make_async_remote_copy(
            src_ref=part.at[k], dst_ref=cur1.at[pl.ds(mine(k) + x * block, block)],
            send_sem=gsend_sem.at[k, i], recv_sem=grecv_sem.at[k, x],
            device_id=(chip(i) * 2 + c, sp), device_id_type=MESH,
        )

    def spread_mate(k, i):
        where = mine(k) + chip(i) * block
        return pltpu.make_async_remote_copy(
            src_ref=part.at[k] if i == 0 else cur1.at[pl.ds(where, block)],
            dst_ref=cur1.at[pl.ds(where, block)],
            send_sem=asend_sem.at[k, i], recv_sem=arecv_sem.at[k, i],
            device_id=(mate, sp), device_id_type=MESH,
        )

    def mean_pair(k):
        to_mate(k).wait_recv()
        xsend[k] = total[pl.ds(mine(k), quarter), :] + crecv[k]
        for i in range(1, nx):
            across(k, i).start()

    def mean_sum(k):
        acc = xsend[k, pl.ds(x * block, block), :]
        for i in range(1, nx):
            pltpu.make_async_remote_copy(
                src_ref=part.at[k], dst_ref=xrecv.at[k, chip(i)],
                send_sem=xsend_sem.at[k, i], recv_sem=xrecv_sem.at[k, chip(i)],
                device_id=(sj, sp), device_id_type=MESH,
            ).wait_recv()
            acc = acc + xrecv[k, chip(i)]
        part[k] = acc * scale
        for i in range(1, nx):
            spread(k, i).start()
        spread_mate(k, 0).start()
        cur1[pl.ds(mine(k) + x * block, block), :] = acc * scale

    def mean_pass(k):
        for i in range(1, nx):
            where = mine(k) + chip(i) * block
            pltpu.make_async_remote_copy(
                src_ref=part.at[k], dst_ref=cur1.at[pl.ds(where, block)],
                send_sem=gsend_sem.at[k, i], recv_sem=grecv_sem.at[k, chip(i)],
                device_id=(sj, sp), device_id_type=MESH,
            ).wait_recv()
            spread_mate(k, i).start()

    def mean_done(k):
        for i in range(nx):
            where = other(k) + chip(i) * block
            pltpu.make_async_remote_copy(
                src_ref=part.at[k], dst_ref=cur1.at[pl.ds(where, block)],
                send_sem=asend_sem.at[k, i], recv_sem=arecv_sem.at[k, i],
                device_id=(sj, sp), device_id_type=MESH,
            ).wait_recv()

    nb = rows // step
    nw = rows // warp_step
    mid = nb // 2

    arrivals(0)
    warp_blocks(0, 0, nw)
    send_edge(0, 0, 0)
    send_edge(0, 1, 0)
    smooth(0, 0, 1, nb - 1)
    arrivals(1)
    warp_blocks(1, nw - 1, nw)
    warp_blocks(1, 0, 1)
    send_edge(0, 0, 1)
    send_edge(0, 1, 1)
    warp_blocks(1, 1, nw - 1)
    smooth(0, 1, 1, mid)
    for s in range(2):
        wait_halo(0, 0, s)
        smooth_edge(0, 0, s)
    to_mate(0).start()
    smooth(0, 1, mid, nb - 1)
    for s in range(2):
        wait_halo(0, 1, s)
        smooth_edge(0, 1, s)
    to_mate(1).start()
    for k in range(2):
        mean_pair(k)
    for k in range(2):
        mean_sum(k)
    for k in range(2):
        mean_pass(k)
    for k in range(2):
        to_mate(k).wait_send()

    mean_done(0)
    for s in range(2):
        send_edge(1, 0, s)
    for s in range(2):
        smooth(1, s, 1, mid - 1)
    mean_done(1)
    for s in range(2):
        send_edge(1, 1, s)
    for s in range(2):
        smooth(1, s, mid - 1, nb - 1)

    def sort_planes(b):
        base = b * step * PLANE
        for cc in range(2):
            for xx in range(nx):
                for p in range(pd):
                    plane = (2 * xx + cc) * pd + p
                    fsend[b, cc, xx, p] = total[pl.ds(base + plane, step, stride=PLANE), :]

    inner_blocks, ends = pl.ds(1, nb - 2), (pl.ds(0, 1), pl.ds(nb - 1, 1))
    pieces = (inner_blocks,) + ends

    def planes_to_mate(n):
        return pltpu.make_async_remote_copy(
            src_ref=fsend.at[pieces[n], 1 - c], dst_ref=frecv.at[pieces[n]],
            send_sem=fsend_sem.at[n], recv_sem=frecv_sem.at[n],
            device_id=(mate, sp), device_id_type=MESH,
        )

    def planes_across(n, i):
        return pltpu.make_async_remote_copy(
            src_ref=fx.at[chip(i), pieces[n]], dst_ref=fxrecv.at[x, pieces[n]],
            send_sem=ysend_sem.at[n, i], recv_sem=yrecv_sem.at[n, x],
            device_id=(chip(i) * 2 + c, sp), device_id_type=MESH,
        )

    def planes_pair(n, blocks):
        planes_to_mate(n).wait_recv()
        for b in blocks:
            for xx in range(nx):
                fx[xx, b] = fsend[b, c, xx] + frecv[b, xx]
        for i in range(1, nx):
            planes_across(n, i).start()

    def planes_sum(n, blocks):
        for i in range(1, nx):
            pltpu.make_async_remote_copy(
                src_ref=fxrecv.at[0, pieces[n]], dst_ref=fxrecv.at[chip(i), pieces[n]],
                send_sem=ysend_sem.at[n, i], recv_sem=yrecv_sem.at[n, chip(i)],
                device_id=(sj, sp), device_id_type=MESH,
            ).wait_recv()
        for b in blocks:
            acc = fx[x, b]
            for i in range(1, nx):
                acc = acc + fxrecv[chip(i), b]
            for p in range(pd):
                tout_ref[pl.ds(b * step * pd + p, step, stride=pd), :] = acc[p] * scale

    for b in range(1, nb - 1):
        sort_planes(b)
    planes_to_mate(0).start()
    for side in range(2):
        for s in range(2):
            wait_halo(1, side, s)
            smooth_edge(1, side, s)
        sort_planes(0 if side == 0 else nb - 1)
        planes_to_mate(1 + side).start()
    planes_pair(0, range(1, nb - 1))
    planes_pair(1, (0,))
    planes_pair(2, (nb - 1,))
    planes_sum(0, range(1, nb - 1))
    planes_sum(1, (0,))
    planes_sum(2, (nb - 1,))

    for i in range(1, ny):
        ask_y(i).wait_send()
    for i in range(1, nz):
        ask_z(i).wait_send()

    def sent_bricks(j, carry):
        brick(0, j).wait_send()
        brick(1, j).wait_send()
        return carry

    lax.fori_loop(1, ns, sent_bricks, 0)

    def sent_planes(i, carry):
        plane_copy(i).wait_send()
        return carry

    lax.fori_loop(1, nj, sent_planes, 0)
    for side in range(2):

        @pl.when(inside(side))
        def _():
            for it in range(2):
                for s in range(2):
                    edge_copy(it, side, s).wait_send()

    for k in range(2):
        for i in range(nx):
            spread_mate(k, i).wait_send()
        for i in range(1, nx):
            across(k, i).wait_send()
            spread(k, i).wait_send()
    for n in range(3):
        planes_to_mate(n).wait_send()
        for i in range(1, nx):
            planes_across(n, i).wait_send()


def body(nj, ny, nz, images, velocity, weights, template, owners, local_rows, tile_counts):
    ns = ny * nz
    nx = nj // 2
    rows = images.shape[1]
    pd = template.shape[1]
    cap = 2 * rows // ns
    slots = ns * cap
    brick = (PLANE, LANES)
    piece = rows // (2 * nj) * PLANE
    step = max(2, rows // 8)
    nb = rows // step
    vmem = pl.BlockSpec(memory_space=pltpu.VMEM)
    smem = pl.BlockSpec(memory_space=pltpu.SMEM)
    away = pl.BlockSpec(memory_space=pltpu.HBM)
    bf16 = jnp.bfloat16
    dma = pltpu.SemaphoreType.DMA
    field, planes = pl.pallas_call(
        functools.partial(kernel, nj, ny, nz, rows, cap),
        out_shape=(
            pltpu.VMEM(velocity.shape, F32),
            jax.ShapeDtypeStruct((rows * pd, LANES), F32),
        ),
        in_specs=[away, away, away, vmem, vmem, vmem, smem],
        out_specs=(vmem, vmem),
        scratch_shapes=[
            pltpu.VMEM((2, rows) + brick, bf16),
            pltpu.VMEM((3, 2, rows) + brick, bf16),
            pltpu.VMEM((2, slots) + brick, bf16),
            pltpu.VMEM((slots,) + brick, bf16),
            pltpu.VMEM((slots,) + brick, bf16),
            pltpu.VMEM((2, rows) + brick, F32),
            pltpu.VMEM((3, 2, rows) + brick, F32),
            pltpu.VMEM((2, rows) + brick, F32),
            pltpu.VMEM((2, rows) + brick, F32),
            pltpu.VMEM((2, rows) + brick, F32),
            pltpu.VMEM((rows * PLANE, LANES), F32),
            pltpu.VMEM((rows * PLANE, LANES), F32),
            pltpu.VMEM((rows * PLANE, LANES), F32),
            pltpu.VMEM((pd, rows, LANES), F32),
            pltpu.VMEM((nj, pd, rows, LANES), F32),
            pltpu.VMEM((ny, nz, 1, LANES), I32),
            pltpu.VMEM((ny, nz, 1, LANES), I32),
            pltpu.VMEM((nz, ny, 1, LANES), I32),
            pltpu.VMEM((2, 1, LANES), I32),
            pltpu.SMEM((nz, ny, 1, LANES), I32),
            pltpu.SMEM((2, 1, LANES), I32),
            pltpu.VMEM((2, 2, 2, 3) + brick, F32),
            pltpu.VMEM((2, 2, 2, 3) + brick, F32),
            pltpu.VMEM((2, piece, LANES), F32),
            pltpu.VMEM((2, rows // 4 * PLANE, LANES), F32),
            pltpu.VMEM((2, rows // 4 * PLANE, LANES), F32),
            pltpu.VMEM((2, nx, piece, LANES), F32),
            pltpu.VMEM((nb, 2, nx, pd, step, LANES), F32),
            pltpu.VMEM((nb, nx, pd, step, LANES), F32),
            pltpu.VMEM((nx, nb, pd, step, LANES), F32),
            pltpu.VMEM((nx, nb, pd, step, LANES), F32),
            dma((3,)), dma((nj,)), dma((nj,)), dma((2, nz)), dma((2, nz)), dma((4,)),
            dma((2, ns)), dma((2, ns)), dma((2, 2, 2)), dma((2, 2, 2)),
            dma((2,)), dma((2,)), dma((2, nx)), dma((2, nx)), dma((2, nx)), dma((2, nx)),
            dma((2, nx)), dma((2, nx)), dma((3,)), dma((3,)), dma((3, nx)), dma((3, nx)),
        ],
        compiler_params=pltpu.CompilerParams(
            collective_id=0, has_side_effects=True, vmem_limit_bytes=62200 * 1024
        ),
        name="demons",
    )(
        images, velocity, weights, template.reshape(rows * pd, LANES),
        jnp.swapaxes(owners, 1, 2), local_rows, tile_counts.T,
    )
    return field, planes.reshape(template.shape)


def solution(mesh):
    nj, ns = mesh.shape["subj"], mesh.shape["space"]
    nz = 8 if ns % 8 == 0 else 2
    in_specs = (
        P("subj", "space", None, None),
        P(None, "subj", "space", None, None),
        P(None, "subj", "space", None, None),
        P("space", "subj", None),
        P("subj", "space", None),
        P("subj", "space"),
        P("subj", "space"),
    )
    out_specs = (P(None, "subj", "space", None, None), P("space", "subj", None))
    return jax.shard_map(
        functools.partial(body, nj, ns // nz, nz),
        mesh=mesh, in_specs=in_specs, out_specs=out_specs, check_vma=False,
    )
```

```python
import functools

import jax
import jax.numpy as jnp
from jax import lax
from jax.experimental import pallas as pl
from jax.experimental.pallas import tpu as pltpu
from jax.sharding import PartitionSpec as P

MESH = pl.DeviceIdType.MESH
F32 = jnp.float32
I32 = jnp.int32
PLANE = 16
LANES = 128


def kernel(
    nj, ny, nz, rows, cap,
    img_h, vel_h, wts_h, tin_ref, own_ref, loc_ref, cnt_ref,
    f, tout_ref,
    img, below0, below1, above0, above1, wts, sendb, recvb0, recvb1, warp, g, q, r, pr, cur0, cur1, total,
    tsend, trecv, req, req_y, req_z, slot_v, rreq_s, slot_s, edge, halo,
    part, crecv, xsend, xrecv, fsend, frecv, fx, fxrecv,
    in_sem, tsend_sem, trecv_sem, qsend_sem, qrecv_sem, loc_sem,
    lsend_sem, lrecv_sem, bsend_sem, brecv_sem, hsend_sem, hrecv_sem,
    csend_sem, crecv_sem, xsend_sem, xrecv_sem, gsend_sem, grecv_sem,
    asend_sem, arecv_sem, fsend_sem, frecv_sem, ysend_sem, yrecv_sem,
):
    ns = ny * nz
    nx = nj // 2
    pd = PLANE // nj
    sj = lax.axis_index("subj")
    sp = lax.axis_index("space")
    x, c = sj // 2, sj % 2
    y, z = sp // nz, sp % nz
    mate = x * 2 + (1 - c)
    recvb = (recvb0, recvb1)
    warp_step = 4 if rows >= 32 else 2
    step = max(2, rows // 8)

    every, even, odd = (0, ny, 1), (0, ny, 2), (1, ny, 2)
    serves = (
        (0, 0, every), (0, -1, every), (0, 1, every),
        (1, -1, every), (2, -1, every), (3, -1, even),
        (-1, 1, every), (-2, 1, every), (-3, 1, odd),
    )
    order = (5, 8, 1, 4, 7, 2, 3, 6, 0)

    img_in = pltpu.make_async_copy(img_h, img, in_sem.at[0])
    img_in.start()
    wts_in = pltpu.make_async_copy(wts_h, wts, in_sem.at[1])
    wts_in.start()
    vel_in = pltpu.make_async_copy(vel_h, f, in_sem.at[2])
    vel_in.start()

    barrier = pltpu.get_barrier_semaphore()

    def along_y(i):
        return ((y + i) % ny) * nz + z

    def along_z(i):
        return y * nz + (z + nz + i) % nz

    for i in range(1, ny):
        pl.semaphore_signal(barrier, inc=1, device_id=(sj, along_y(i)), device_id_type=MESH)
    for e in range(3, 9):
        pl.semaphore_signal(barrier, inc=1, device_id=(sj, along_z(serves[e][0])), device_id_type=MESH)

    def greet_subj(i, carry):
        pl.semaphore_signal(barrier, inc=1, device_id=((sj + i) % nj, sp), device_id_type=MESH)
        return carry

    lax.fori_loop(1, nj, greet_subj, 0)

    for p in range(pd):
        tsend[p] = tin_ref[pl.ds(p, rows, stride=pd), :]

    i0 = lax.broadcasted_iota(I32, (rows, rows), 0)
    i1 = lax.broadcasted_iota(I32, (rows, rows), 1)
    who = lax.broadcasted_iota(I32, (ns, rows), 0)
    lane = lax.broadcasted_iota(I32, (ns, LANES), 1)
    asked = jnp.zeros((ns, LANES), I32)
    slot_v[...] = jnp.zeros_like(slot_v)
    for s in range(2):
        count = cnt_ref[0, s]
        first = count // 2
        last = rows - (count - first)
        row = own_ref[s]
        col = jnp.sum(jnp.where(i0 == i1, row, 0), axis=1, keepdims=True)
        alive0 = (i0 < first) | (i0 >= last)
        hit = (col == row) & (i0 < i1) & alive0
        before = jnp.sum(jnp.where(hit, 1, 0), axis=0, keepdims=True)
        t1 = i1[0:1, :]
        alive1 = (t1 < first) | (t1 >= last)
        slot = jnp.where(alive1, row * cap + before, 0)
        slot_v[s, :, 0:rows] = slot
        place = jnp.where(alive1, before, cap)
        for k in range(cap):
            mine = (row == who) & (place == k)
            column = jnp.sum(jnp.where(mine, loc_ref[s : s + 1, :], 0), axis=1, keepdims=True)
            asked = asked + jnp.where(lane == s * cap + k, column, 0)
    for d in range(ns):
        req[d // nz, d % nz] = asked[d : d + 1, :]
    slots_in = pltpu.make_async_copy(slot_v, slot_s, loc_sem.at[0])
    slots_in.start()

    pl.semaphore_wait(barrier, ny - 1 + 6 + nj - 1)

    def ask_y(i):
        return pltpu.make_async_remote_copy(
            src_ref=req.at[(y + i) % ny], dst_ref=req_y.at[y],
            send_sem=qsend_sem.at[0, i], recv_sem=qrecv_sem.at[0, y],
            device_id=(sj, along_y(i)), device_id_type=MESH,
        )

    def asked_y(i):
        return pltpu.make_async_remote_copy(
            src_ref=req.at[0], dst_ref=req_y.at[(y + i) % ny],
            send_sem=qsend_sem.at[0, i], recv_sem=qrecv_sem.at[0, (y + i) % ny],
            device_id=(sj, sp), device_id_type=MESH,
        )

    def ask_z(e):
        back, image, _ = serves[e]
        return pltpu.make_async_remote_copy(
            src_ref=req_y.at[:, (z + nz - back + image) % nz], dst_ref=req_z.at[e],
            send_sem=qsend_sem.at[1, e], recv_sem=qrecv_sem.at[1, e],
            device_id=(sj, along_z(-back)), device_id_type=MESH,
        )

    def asked_z(e):
        return pltpu.make_async_remote_copy(
            src_ref=req_y.at[:, 0], dst_ref=req_z.at[e],
            send_sem=qsend_sem.at[1, e], recv_sem=qrecv_sem.at[1, e],
            device_id=(sj, sp), device_id_type=MESH,
        )

    below, above = (below0, below1), (above0, above1)

    def lend(s, side):
        return pltpu.make_async_remote_copy(
            src_ref=img.at[s], dst_ref=below[s] if side == 0 else above[s],
            send_sem=lsend_sem.at[s, side], recv_sem=lrecv_sem.at[s, side],
            device_id=(sj, along_z(1 if side == 0 else -1)), device_id_type=MESH,
        )

    def lent(s, side):
        return pltpu.make_async_remote_copy(
            src_ref=img.at[s], dst_ref=below[s] if side == 0 else above[s],
            send_sem=lsend_sem.at[s, side], recv_sem=lrecv_sem.at[s, side],
            device_id=(sj, sp), device_id_type=MESH,
        )

    for i in range(1, ny):
        ask_y(i).start()
    img_in.wait()
    lend(0, 0).start()
    lend(0, 1).start()
    req_y[y] = req[y]
    for i in range(1, ny):
        asked_y(i).wait_recv()
    for e in (5, 8, 4, 7, 3, 6):
        ask_z(e).start()
    lend(1, 0).start()
    lend(1, 1).start()
    for e in range(3):
        for n in range(ny):
            req_z[e, n] = req_y[n, (z + nz + serves[e][1]) % nz]

    def plane_copy(i):
        return pltpu.make_async_remote_copy(
            src_ref=tsend, dst_ref=trecv.at[sj],
            send_sem=tsend_sem.at[i], recv_sem=trecv_sem.at[sj],
            device_id=((sj + i) % nj, sp), device_id_type=MESH,
        )

    def start_planes(i, carry):
        plane_copy(i).start()
        return carry

    lax.fori_loop(1, nj, start_planes, 0)

    for e in range(3, 9):
        asked_z(e).wait_recv()
    rreq_in = pltpu.make_async_copy(req_z, rreq_s, loc_sem.at[2])
    rreq_in.start()
    rreq_in.wait()

    def owner_of(e):
        return y * nz + (z + nz + serves[e][1]) % nz

    def brick(s, e, dy):
        d = ((y + dy) % ny) * nz + (z + nz + serves[e][0]) % nz
        return pltpu.make_async_remote_copy(
            src_ref=sendb.at[s, pl.ds((e * ny + dy) * cap, cap)],
            dst_ref=recvb[s].at[pl.ds(owner_of(e) * cap, cap)],
            send_sem=bsend_sem.at[s, e * ny + dy], recv_sem=brecv_sem.at[s, owner_of(e)],
            device_id=(sj, d), device_id_type=MESH,
        )

    def brick_from(s, d):
        return pltpu.make_async_remote_copy(
            src_ref=sendb.at[s, pl.ds(0, cap)], dst_ref=recvb[s].at[pl.ds(d * cap, cap)],
            send_sem=bsend_sem.at[s, 0], recv_sem=brecv_sem.at[s, d],
            device_id=(sj, sp), device_id_type=MESH,
        )

    def over_y(e, what):
        first, last, stride = serves[e][2]
        first = first + stride if serves[e][0] == 0 else first
        count = len(range(first, last, stride))

        def one(i, carry):
            what(first + i * stride)
            return carry

        if count:
            lax.fori_loop(0, count, one, 0)

    def wanted(s, e, dy, k):
        where = rreq_s[e, (y + dy) % ny, 0, s * cap + k]
        if serves[e][1] == 0:
            return img[s, where]
        return below[s][where] if serves[e][1] < 0 else above[s][where]

    for s in range(2):
        lent(s, 0).wait_recv()
        lent(s, 1).wait_recv()
        started = None
        for e in order:

            def gather(dy, s=s, e=e):
                for k in range(cap):
                    sendb[s, (e * ny + dy) * cap + k] = wanted(s, e, dy, k)

            over_y(e, gather)
            if started is not None:
                over_y(started, lambda dy, s=s, e=started: brick(s, e, dy).start())
            started = e
        for e in range(3):
            for k in range(cap):
                recvb[s][owner_of(e) * cap + k] = wanted(s, e, 0, k)
        over_y(started, lambda dy, s=s, e=started: brick(s, e, dy).start())

    def wait_planes(i, carry):
        other = (sj + i) % nj
        pltpu.make_async_remote_copy(
            src_ref=tsend, dst_ref=trecv.at[other],
            send_sem=tsend_sem.at[0], recv_sem=trecv_sem.at[other],
            device_id=(sj, sp), device_id_type=MESH,
        ).wait_recv()
        return carry

    lax.fori_loop(1, nj, wait_planes, 0)
    trecv[sj] = tsend[...]
    for j in range(nj):
        for p in range(pd):
            cur0[pl.ds(j * pd + p, rows, stride=PLANE), :] = trecv[j, p]

    @pl.when(sp == 0)
    def _():
        halo[:, 0] = jnp.zeros_like(halo[:, 0])

    @pl.when(sp == ns - 1)
    def _():
        halo[:, 1] = jnp.zeros_like(halo[:, 1])

    wts_in.wait()
    vel_in.wait()
    slots_in.wait()

    lanes = lax.broadcasted_iota(I32, (8, LANES), 1)
    subs = lax.broadcasted_iota(I32, (8, LANES), 0)
    low = subs < 4
    y_top = subs % 4 == 3
    y_bot = subs % 4 == 0
    z_top = lanes == LANES - 1
    z_bot = lanes == 0

    def up_z(v):
        return jnp.where(z_top, 0.0, pltpu.roll(v, LANES - 1, 1))

    def down_z(v):
        return jnp.where(z_bot, 0.0, pltpu.roll(v, 1, 1))

    def up_y(v):
        return jnp.where(y_top, 0.0, pltpu.roll(v, 7, 0))

    def down_y(v):
        return jnp.where(y_bot, 0.0, pltpu.roll(v, 1, 0))

    def up_x(pair):
        a, b = [pltpu.roll(v, 4, 0) for v in pair]
        return [jnp.where(low, a, b), jnp.where(low, b, 0.0)]

    def pair_of(value):
        return [value[0:8], value[8:16]]

    def put(ref, index, pair):
        ref[index + (slice(0, 8),)] = pair[0]
        ref[index + (slice(8, 16),)] = pair[1]

    both = (0, 1)

    def arrivals(s):
        def far(n, carry):
            brick_from(s, ((y + 1 + n // nz) % ny) * nz + n % nz).wait_recv()
            return carry

        def near(n, carry):
            brick_from(s, y * nz + (z + n) % nz).wait_recv()
            return carry

        lax.fori_loop(0, (ny - 1) * nz, far, 0)
        lax.fori_loop(2, nz - 1, near, 0)

    def warp_blocks(s, start, stop):
        count = cnt_ref[0, s]
        first = count // 2
        last = rows - (count - first)

        def warp_tile(t):
            b00 = pair_of(recvb[s][slot_s[s, 0, t]].astype(F32))
            wx, wy, wz = [pair_of(wts[a, s, t].astype(F32)) for a in range(3)]
            live = jnp.where((t < first) | (t >= last), 1.0, 0.0).astype(F32)
            d00 = [up_z(v) - v for v in b00]
            b01, d01 = [up_y(v) for v in b00], [up_y(v) for v in d00]
            b10, d10 = up_x(b00), up_x(d00)
            b11, d11 = up_x(b01), up_x(d01)
            w = []
            for i in both:
                l00 = b00[i] + wz[i] * d00[i]
                l01 = b01[i] + wz[i] * d01[i]
                l10 = b10[i] + wz[i] * d10[i]
                l11 = b11[i] + wz[i] * d11[i]
                m0 = l00 + wy[i] * (l01 - l00)
                m1 = l10 + wy[i] * (l11 - l10)
                w.append((m0 + wx[i] * (m1 - m0)) * live)
            h = [0.5 * v for v in w]
            ra, rb = [pltpu.roll(v, 4, 0) for v in h]
            mid = jnp.where(low, ra, rb)
            gx = [mid - jnp.where(low, 0.0, ra), jnp.where(low, rb, 0.0) - mid]
            gy = [up_y(v) - down_y(v) for v in h]
            gz = [up_z(v) - down_z(v) for v in h]
            here = pl.multiple_of(t * PLANE, PLANE)
            now = pair_of(cur0[pl.ds(here, PLANE), :])
            fx0, fy0, fz0 = [pair_of(f[a, s, t]) for a in range(3)]
            qq, rr = [], []
            for i in both:
                sq = gx[i] * gx[i] + gy[i] * gy[i] + gz[i] * gz[i]
                inverse = 1.0 / (16.0 * sq + 4.0)
                pred = w[i] + (gx[i] * fx0[i] + gy[i] * fy0[i]) + gz[i] * fz0[i]
                qq.append(inverse)
                rr.append((pred - now[i]) * inverse)
            put(warp, (s, t), w)
            put(g, (0, s, t), gx)
            put(g, (1, s, t), gy)
            put(g, (2, s, t), gz)
            put(q, (s, t), qq)
            put(r, (s, t), rr)

        def warp_block(b, carry):
            for n in range(warp_step):
                warp_tile(b * warp_step + n)
            return carry

        lax.fori_loop(start, stop, warp_block, 0)

    def first_ratio(s, t):
        return pair_of(r[s, t])

    def second_ratio(s, t):
        here = pl.multiple_of(t * PLANE, PLANE)
        now = pair_of(cur1[pl.ds(here, PLANE), :])
        p1 = pair_of(pr[s, t])
        qq = pair_of(q[s, t])
        return [(p1[i] - now[i]) * qq[i] for i in both]

    def edge_copy(it, side, s):
        d = sp - 1 if side == 0 else sp + 1
        return pltpu.make_async_remote_copy(
            src_ref=edge.at[it, side, s], dst_ref=halo.at[it, 1 - side, s],
            send_sem=hsend_sem.at[it, side, s], recv_sem=hrecv_sem.at[it, 1 - side, s],
            device_id=(sj, d), device_id_type=MESH,
        )

    def halo_in(it, side, s):
        return pltpu.make_async_remote_copy(
            src_ref=edge.at[it, side, s], dst_ref=halo.at[it, side, s],
            send_sem=hsend_sem.at[it, side, s], recv_sem=hrecv_sem.at[it, side, s],
            device_id=(sj, sp), device_id_type=MESH,
        )

    def inside(side):
        return sp > 0 if side == 0 else sp < ns - 1

    def update(it, s, t):
        rr = first_ratio(s, t) if it == 0 else second_ratio(s, t)
        out = []
        for a in range(3):
            gg = pair_of(g[a, s, t])
            out += [gg[0] * rr[0], gg[1] * rr[1]]
        return out

    def send_edge(it, side, s):
        u = update(it, s, 0 if side == 0 else rows - 1)
        for a in range(3):
            put(edge, (it, side, s, a), u[2 * a : 2 * a + 2])

        @pl.when(inside(side))
        def _():
            edge_copy(it, side, s).start()

    def wait_halo(it, side, s):
        @pl.when(inside(side))
        def _():
            halo_in(it, side, s).wait_recv()

    def advance(it, s, t, v):
        new = []
        for a in range(3):
            old = pair_of(f[a, s, t])
            out = []
            for i in both:
                value = v[2 * a + i]
                two = value + down_z(value)
                out.append(old[i] - (two + jnp.where(z_top, value, pltpu.roll(two, LANES - 1, 1))))
            put(f, (a, s, t), out)
            new.append(out)
        w = pair_of(warp[s, t])
        gg = [pair_of(g[a, s, t]) for a in range(3)]
        pred = [
            w[i] + (gg[0][i] * new[0][i] + gg[1][i] * new[1][i]) + gg[2][i] * new[2][i]
            for i in both
        ]
        if it == 0:
            put(pr, (s, t), pred)
        here = pl.multiple_of(t * PLANE, PLANE)
        if s == 0:
            total[pl.ds(here, 8), :] = pred[0]
            total[pl.ds(here + 8, 8), :] = pred[1]
        else:
            total[pl.ds(here, 8), :] = total[pl.ds(here, 8), :] + pred[0]
            total[pl.ds(here + 8, 8), :] = total[pl.ds(here + 8, 8), :] + pred[1]

    def add(p, o):
        return [a + b for a, b in zip(p, o)]

    def run(it, s, start, low_row, high_row):
        u = update(it, s, start)
        two = add(low_row or update(it, s, start - 1), u)
        for n in range(step):
            at_end = n == step - 1
            after = high_row if at_end and high_row else update(it, s, start + n + 1)
            ahead = add(u, after)
            advance(it, s, start + n, add(two, ahead))
            u, two = after, ahead

    def smooth(it, s, start, stop):
        def inner(b, carry):
            run(it, s, b * step, None, None)
            return carry

        lax.fori_loop(start, stop, inner, 0)

    def smooth_edge(it, side, s):
        far = []
        for a in range(3):
            far += pair_of(halo[it, side, s, a])
        if side == 0:
            run(it, s, 0, far, None)
        else:
            run(it, s, rows - step, None, far)

    def chip(i):
        return (x + i) % nx

    quarter = rows // 4 * PLANE
    block = rows // (2 * nj) * PLANE
    scale = 1.0 / (2.0 * nj)

    def mine(k):
        return (2 * k + c) * quarter

    def other(k):
        return (2 * k + 1 - c) * quarter

    def to_mate(k):
        return pltpu.make_async_remote_copy(
            src_ref=total.at[pl.ds(other(k), quarter)], dst_ref=crecv.at[k],
            send_sem=csend_sem.at[k], recv_sem=crecv_sem.at[k],
            device_id=(mate, sp), device_id_type=MESH,
        )

    def across(k, i):
        return pltpu.make_async_remote_copy(
            src_ref=xsend.at[k, pl.ds(chip(i) * block, block)], dst_ref=xrecv.at[k, x],
            send_sem=xsend_sem.at[k, i], recv_sem=xrecv_sem.at[k, x],
            device_id=(chip(i) * 2 + c, sp), device_id_type=MESH,
        )

    def spread(k, i):
        return pltpu.make_async_remote_copy(
            src_ref=part.at[k], dst_ref=cur1.at[pl.ds(mine(k) + x * block, block)],
            send_sem=gsend_sem.at[k, i], recv_sem=grecv_sem.at[k, x],
            device_id=(chip(i) * 2 + c, sp), device_id_type=MESH,
        )

    def spread_mate(k, i):
        where = mine(k) + chip(i) * block
        return pltpu.make_async_remote_copy(
            src_ref=part.at[k] if i == 0 else cur1.at[pl.ds(where, block)],
            dst_ref=cur1.at[pl.ds(where, block)],
            send_sem=asend_sem.at[k, i], recv_sem=arecv_sem.at[k, i],
            device_id=(mate, sp), device_id_type=MESH,
        )

    def mean_pair(k):
        to_mate(k).wait_recv()
        xsend[k] = total[pl.ds(mine(k), quarter), :] + crecv[k]
        for i in range(1, nx):
            across(k, i).start()

    def mean_sum(k):
        acc = xsend[k, pl.ds(x * block, block), :]
        for i in range(1, nx):
            pltpu.make_async_remote_copy(
                src_ref=part.at[k], dst_ref=xrecv.at[k, chip(i)],
                send_sem=xsend_sem.at[k, i], recv_sem=xrecv_sem.at[k, chip(i)],
                device_id=(sj, sp), device_id_type=MESH,
            ).wait_recv()
            acc = acc + xrecv[k, chip(i)]
        part[k] = acc * scale
        for i in range(1, nx):
            spread(k, i).start()
        spread_mate(k, 0).start()
        cur1[pl.ds(mine(k) + x * block, block), :] = acc * scale

    def mean_pass(k):
        for i in range(1, nx):
            where = mine(k) + chip(i) * block
            pltpu.make_async_remote_copy(
                src_ref=part.at[k], dst_ref=cur1.at[pl.ds(where, block)],
                send_sem=gsend_sem.at[k, i], recv_sem=grecv_sem.at[k, chip(i)],
                device_id=(sj, sp), device_id_type=MESH,
            ).wait_recv()
            spread_mate(k, i).start()

    def mean_done(k):
        for i in range(nx):
            where = other(k) + chip(i) * block
            pltpu.make_async_remote_copy(
                src_ref=part.at[k], dst_ref=cur1.at[pl.ds(where, block)],
                send_sem=asend_sem.at[k, i], recv_sem=arecv_sem.at[k, i],
                device_id=(sj, sp), device_id_type=MESH,
            ).wait_recv()

    nb = rows // step
    nw = rows // warp_step
    mid = nb // 2

    arrivals(0)
    warp_blocks(0, 0, nw)
    send_edge(0, 0, 0)
    send_edge(0, 1, 0)
    smooth(0, 0, 1, nb - 1)
    arrivals(1)
    warp_blocks(1, nw - 1, nw)
    warp_blocks(1, 0, 1)
    send_edge(0, 0, 1)
    send_edge(0, 1, 1)
    warp_blocks(1, 1, nw - 1)
    smooth(0, 1, 1, mid)
    for s in range(2):
        wait_halo(0, 0, s)
        smooth_edge(0, 0, s)
    to_mate(0).start()
    smooth(0, 1, mid, nb - 1)
    for s in range(2):
        wait_halo(0, 1, s)
        smooth_edge(0, 1, s)
    to_mate(1).start()
    for k in range(2):
        mean_pair(k)
    for k in range(2):
        mean_sum(k)
    for k in range(2):
        mean_pass(k)
    for k in range(2):
        to_mate(k).wait_send()

    mean_done(0)
    for s in range(2):
        send_edge(1, 0, s)
    for s in range(2):
        smooth(1, s, 1, mid - 1)
    mean_done(1)
    for s in range(2):
        send_edge(1, 1, s)
    for s in range(2):
        smooth(1, s, mid - 1, nb - 1)

    def sort_planes(b):
        base = b * step * PLANE
        for cc in range(2):
            for xx in range(nx):
                for p in range(pd):
                    plane = (2 * xx + cc) * pd + p
                    fsend[b, cc, xx, p] = total[pl.ds(base + plane, step, stride=PLANE), :]

    inner_blocks, ends = pl.ds(1, nb - 2), (pl.ds(0, 1), pl.ds(nb - 1, 1))
    pieces = (inner_blocks,) + ends

    def planes_to_mate(n):
        return pltpu.make_async_remote_copy(
            src_ref=fsend.at[pieces[n], 1 - c], dst_ref=frecv.at[pieces[n]],
            send_sem=fsend_sem.at[n], recv_sem=frecv_sem.at[n],
            device_id=(mate, sp), device_id_type=MESH,
        )

    def planes_across(n, i):
        return pltpu.make_async_remote_copy(
            src_ref=fx.at[chip(i), pieces[n]], dst_ref=fxrecv.at[x, pieces[n]],
            send_sem=ysend_sem.at[n, i], recv_sem=yrecv_sem.at[n, x],
            device_id=(chip(i) * 2 + c, sp), device_id_type=MESH,
        )

    def planes_pair(n, blocks):
        planes_to_mate(n).wait_recv()
        for b in blocks:
            for xx in range(nx):
                fx[xx, b] = fsend[b, c, xx] + frecv[b, xx]
        for i in range(1, nx):
            planes_across(n, i).start()

    def planes_sum(n, blocks):
        for i in range(1, nx):
            pltpu.make_async_remote_copy(
                src_ref=fxrecv.at[0, pieces[n]], dst_ref=fxrecv.at[chip(i), pieces[n]],
                send_sem=ysend_sem.at[n, i], recv_sem=yrecv_sem.at[n, chip(i)],
                device_id=(sj, sp), device_id_type=MESH,
            ).wait_recv()
        for b in blocks:
            acc = fx[x, b]
            for i in range(1, nx):
                acc = acc + fxrecv[chip(i), b]
            for p in range(pd):
                tout_ref[pl.ds(b * step * pd + p, step, stride=pd), :] = acc[p] * scale

    for b in range(1, nb - 1):
        sort_planes(b)
    planes_to_mate(0).start()
    for side in range(2):
        for s in range(2):
            wait_halo(1, side, s)
            smooth_edge(1, side, s)
        sort_planes(0 if side == 0 else nb - 1)
        planes_to_mate(1 + side).start()
    planes_pair(0, range(1, nb - 1))
    planes_pair(1, (0,))
    planes_pair(2, (nb - 1,))
    planes_sum(0, range(1, nb - 1))
    planes_sum(1, (0,))
    planes_sum(2, (nb - 1,))

    for i in range(1, ny):
        ask_y(i).wait_send()
    for e in range(3, 9):
        ask_z(e).wait_send()
    for s in range(2):
        lend(s, 0).wait_send()
        lend(s, 1).wait_send()
        for e in order:
            over_y(e, lambda dy, s=s, e=e: brick(s, e, dy).wait_send())

    def sent_planes(i, carry):
        plane_copy(i).wait_send()
        return carry

    lax.fori_loop(1, nj, sent_planes, 0)
    for side in range(2):

        @pl.when(inside(side))
        def _():
            for it in range(2):
                for s in range(2):
                    edge_copy(it, side, s).wait_send()

    for k in range(2):
        for i in range(nx):
            spread_mate(k, i).wait_send()
        for i in range(1, nx):
            across(k, i).wait_send()
            spread(k, i).wait_send()
    for n in range(3):
        planes_to_mate(n).wait_send()
        for i in range(1, nx):
            planes_across(n, i).wait_send()


def body(nj, ny, nz, images, velocity, weights, template, owners, local_rows, tile_counts):
    ns = ny * nz
    nx = nj // 2
    rows = images.shape[1]
    pd = template.shape[1]
    cap = 2 * rows // ns
    slots = ns * cap
    brick = (PLANE, LANES)
    piece = rows // (2 * nj) * PLANE
    step = max(2, rows // 8)
    nb = rows // step
    vmem = pl.BlockSpec(memory_space=pltpu.VMEM)
    smem = pl.BlockSpec(memory_space=pltpu.SMEM)
    away = pl.BlockSpec(memory_space=pltpu.HBM)
    bf16 = jnp.bfloat16
    dma = pltpu.SemaphoreType.DMA
    field, planes = pl.pallas_call(
        functools.partial(kernel, nj, ny, nz, rows, cap),
        out_shape=(
            pltpu.VMEM(velocity.shape, F32),
            jax.ShapeDtypeStruct((rows * pd, LANES), F32),
        ),
        in_specs=[away, away, away, vmem, vmem, vmem, smem],
        out_specs=(vmem, vmem),
        scratch_shapes=[
            pltpu.VMEM((2, rows) + brick, bf16),
            pltpu.VMEM((rows,) + brick, bf16),
            pltpu.VMEM((rows,) + brick, bf16),
            pltpu.VMEM((rows,) + brick, bf16),
            pltpu.VMEM((rows,) + brick, bf16),
            pltpu.VMEM((3, 2, rows) + brick, bf16),
            pltpu.VMEM((2, 9 * ny * cap) + brick, bf16),
            pltpu.VMEM((slots,) + brick, bf16),
            pltpu.VMEM((slots,) + brick, bf16),
            pltpu.VMEM((2, rows) + brick, F32),
            pltpu.VMEM((3, 2, rows) + brick, F32),
            pltpu.VMEM((2, rows) + brick, F32),
            pltpu.VMEM((2, rows) + brick, F32),
            pltpu.VMEM((2, rows) + brick, F32),
            pltpu.VMEM((rows * PLANE, LANES), F32),
            pltpu.VMEM((rows * PLANE, LANES), F32),
            pltpu.VMEM((rows * PLANE, LANES), F32),
            pltpu.VMEM((pd, rows, LANES), F32),
            pltpu.VMEM((nj, pd, rows, LANES), F32),
            pltpu.VMEM((ny, nz, 1, LANES), I32),
            pltpu.VMEM((ny, nz, 1, LANES), I32),
            pltpu.VMEM((9, ny, 1, LANES), I32),
            pltpu.VMEM((2, 1, LANES), I32),
            pltpu.SMEM((9, ny, 1, LANES), I32),
            pltpu.SMEM((2, 1, LANES), I32),
            pltpu.VMEM((2, 2, 2, 3) + brick, F32),
            pltpu.VMEM((2, 2, 2, 3) + brick, F32),
            pltpu.VMEM((2, piece, LANES), F32),
            pltpu.VMEM((2, rows // 4 * PLANE, LANES), F32),
            pltpu.VMEM((2, rows // 4 * PLANE, LANES), F32),
            pltpu.VMEM((2, nx, piece, LANES), F32),
            pltpu.VMEM((nb, 2, nx, pd, step, LANES), F32),
            pltpu.VMEM((nb, nx, pd, step, LANES), F32),
            pltpu.VMEM((nx, nb, pd, step, LANES), F32),
            pltpu.VMEM((nx, nb, pd, step, LANES), F32),
            dma((3,)), dma((nj,)), dma((nj,)), dma((2, 9)), dma((2, 9)), dma((4,)),
            dma((2, 2)), dma((2, 2)), dma((2, 9 * ny)), dma((2, ns)), dma((2, 2, 2)), dma((2, 2, 2)),
            dma((2,)), dma((2,)), dma((2, nx)), dma((2, nx)), dma((2, nx)), dma((2, nx)),
            dma((2, nx)), dma((2, nx)), dma((3,)), dma((3,)), dma((3, nx)), dma((3, nx)),
        ],
        compiler_params=pltpu.CompilerParams(
            collective_id=0, has_side_effects=True, vmem_limit_bytes=62200 * 1024
        ),
        name="demons",
    )(
        images, velocity, weights, template.reshape(rows * pd, LANES),
        jnp.swapaxes(owners, 1, 2), local_rows, tile_counts.T,
    )
    return field, planes.reshape(template.shape)


def solution(mesh):
    nj, ns = mesh.shape["subj"], mesh.shape["space"]
    nz = 8 if ns % 8 == 0 else 2
    in_specs = (
        P("subj", "space", None, None),
        P(None, "subj", "space", None, None),
        P(None, "subj", "space", None, None),
        P("space", "subj", None),
        P("subj", "space", None),
        P("subj", "space"),
        P("subj", "space"),
    )
    out_specs = (P(None, "subj", "space", None, None), P("space", "subj", None))
    return jax.shard_map(
        functools.partial(body, nj, ns // nz, nz),
        mesh=mesh, in_specs=in_specs, out_specs=out_specs, check_vma=False,
    )
```

```python
import functools

import jax
import jax.numpy as jnp
from jax import lax
from jax.experimental import pallas as pl
from jax.experimental.pallas import tpu as pltpu
from jax.sharding import PartitionSpec as P

MESH = pl.DeviceIdType.MESH
F32 = jnp.float32
I32 = jnp.int32
PLANE = 16
LANES = 128


def kernel(
    nj, ny, nz, rows, cap,
    img_h, vel_h, wts_h, tin_ref, own_ref, loc_ref, cnt_ref,
    f, tout_ref,
    img, below0, below1, above0, above1, wts, sendb, recvb0, recvb1, warp, g, q, r, pr, cur0, cur1, total,
    tsend, trecv, req, req_y, req_z, slot_v, rreq_s, slot_s, edge, halo,
    part, crecv, xsend, xrecv, fsend, frecv, fx, fxrecv,
    in_sem, tsend_sem, trecv_sem, qsend_sem, qrecv_sem, loc_sem,
    lsend_sem, lrecv_sem, bsend_sem, brecv_sem, hsend_sem, hrecv_sem,
    csend_sem, crecv_sem, xsend_sem, xrecv_sem, gsend_sem, grecv_sem,
    asend_sem, arecv_sem, fsend_sem, frecv_sem, ysend_sem, yrecv_sem,
):
    ns = ny * nz
    nx = nj // 2
    pd = PLANE // nj
    sj = lax.axis_index("subj")
    sp = lax.axis_index("space")
    x, c = sj // 2, sj % 2
    y, z = sp // nz, sp % nz
    mate = x * 2 + (1 - c)
    recvb = (recvb0, recvb1)
    warp_step = 8 if rows >= 32 else 2
    step = max(2, rows // 8)

    every, even, odd = (0, ny, 1), (0, ny, 2), (1, ny, 2)
    serves = (
        (0, 0, every), (0, -1, every), (0, 1, every),
        (1, -1, every), (2, -1, every), (3, -1, even),
        (-1, 1, every), (-2, 1, every), (-3, 1, odd),
    )
    order = ((1, 2, 0, 5, 8, 4, 7, 3, 6), (5, 8, 4, 7, 3, 6, 1, 2, 0))

    img_in = pltpu.make_async_copy(img_h, img, in_sem.at[0])
    img_in.start()
    wts_in = pltpu.make_async_copy(wts_h, wts, in_sem.at[1])
    wts_in.start()
    vel_in = pltpu.make_async_copy(vel_h, f, in_sem.at[2])
    vel_in.start()

    barrier = pltpu.get_barrier_semaphore()

    def along_y(i):
        return ((y + i) % ny) * nz + z

    def along_z(i):
        return y * nz + (z + nz + i) % nz

    for i in range(1, ny):
        pl.semaphore_signal(barrier, inc=1, device_id=(sj, along_y(i)), device_id_type=MESH)
    for e in range(3, 9):
        pl.semaphore_signal(barrier, inc=1, device_id=(sj, along_z(serves[e][0])), device_id_type=MESH)

    def greet_subj(i, carry):
        pl.semaphore_signal(barrier, inc=1, device_id=((sj + i) % nj, sp), device_id_type=MESH)
        return carry

    lax.fori_loop(1, nj, greet_subj, 0)

    for p in range(pd):
        tsend[p] = tin_ref[pl.ds(p, rows, stride=pd), :]

    i0 = lax.broadcasted_iota(I32, (rows, rows), 0)
    i1 = lax.broadcasted_iota(I32, (rows, rows), 1)
    who = lax.broadcasted_iota(I32, (ns, rows), 0)
    lane = lax.broadcasted_iota(I32, (ns, LANES), 1)
    asked = jnp.zeros((ns, LANES), I32)
    slot_v[...] = jnp.zeros_like(slot_v)
    for s in range(2):
        count = cnt_ref[0, s]
        first = count // 2
        last = rows - (count - first)
        row = own_ref[s]
        col = jnp.sum(jnp.where(i0 == i1, row, 0), axis=1, keepdims=True)
        alive0 = (i0 < first) | (i0 >= last)
        hit = (col == row) & (i0 < i1) & alive0
        before = jnp.sum(jnp.where(hit, 1, 0), axis=0, keepdims=True)
        t1 = i1[0:1, :]
        alive1 = (t1 < first) | (t1 >= last)
        slot = jnp.where(alive1, row * cap + before, 0)
        slot_v[s, :, 0:rows] = slot
        place = jnp.where(alive1, before, cap)
        for k in range(cap):
            mine = (row == who) & (place == k)
            column = jnp.sum(jnp.where(mine, loc_ref[s : s + 1, :], 0), axis=1, keepdims=True)
            asked = asked + jnp.where(lane == s * cap + k, column, 0)
    for d in range(ns):
        req[d // nz, d % nz] = asked[d : d + 1, :]
    slots_in = pltpu.make_async_copy(slot_v, slot_s, loc_sem.at[0])
    slots_in.start()

    pl.semaphore_wait(barrier, ny - 1 + 6 + nj - 1)

    def ask_y(i):
        return pltpu.make_async_remote_copy(
            src_ref=req.at[(y + i) % ny], dst_ref=req_y.at[y],
            send_sem=qsend_sem.at[0, i], recv_sem=qrecv_sem.at[0, y],
            device_id=(sj, along_y(i)), device_id_type=MESH,
        )

    def asked_y(i):
        return pltpu.make_async_remote_copy(
            src_ref=req.at[0], dst_ref=req_y.at[(y + i) % ny],
            send_sem=qsend_sem.at[0, i], recv_sem=qrecv_sem.at[0, (y + i) % ny],
            device_id=(sj, sp), device_id_type=MESH,
        )

    def ask_z(e):
        back, image, _ = serves[e]
        return pltpu.make_async_remote_copy(
            src_ref=req_y.at[:, (z + nz - back + image) % nz], dst_ref=req_z.at[e],
            send_sem=qsend_sem.at[1, e], recv_sem=qrecv_sem.at[1, e],
            device_id=(sj, along_z(-back)), device_id_type=MESH,
        )

    def asked_z(e):
        return pltpu.make_async_remote_copy(
            src_ref=req_y.at[:, 0], dst_ref=req_z.at[e],
            send_sem=qsend_sem.at[1, e], recv_sem=qrecv_sem.at[1, e],
            device_id=(sj, sp), device_id_type=MESH,
        )

    below, above = (below0, below1), (above0, above1)

    def lend(s, side):
        return pltpu.make_async_remote_copy(
            src_ref=img.at[s], dst_ref=below[s] if side == 0 else above[s],
            send_sem=lsend_sem.at[s, side], recv_sem=lrecv_sem.at[s, side],
            device_id=(sj, along_z(1 if side == 0 else -1)), device_id_type=MESH,
        )

    def lent(s, side):
        return pltpu.make_async_remote_copy(
            src_ref=img.at[s], dst_ref=below[s] if side == 0 else above[s],
            send_sem=lsend_sem.at[s, side], recv_sem=lrecv_sem.at[s, side],
            device_id=(sj, sp), device_id_type=MESH,
        )

    for i in range(1, ny):
        ask_y(i).start()
    img_in.wait()
    lend(0, 0).start()
    lend(0, 1).start()
    req_y[y] = req[y]
    for i in range(1, ny):
        asked_y(i).wait_recv()
    for e in (5, 8, 4, 7, 3, 6):
        ask_z(e).start()
    lend(1, 0).start()
    lend(1, 1).start()
    for e in range(3):
        for n in range(ny):
            req_z[e, n] = req_y[n, (z + nz + serves[e][1]) % nz]

    def plane_copy(i):
        return pltpu.make_async_remote_copy(
            src_ref=tsend, dst_ref=trecv.at[sj],
            send_sem=tsend_sem.at[i], recv_sem=trecv_sem.at[sj],
            device_id=((sj + i) % nj, sp), device_id_type=MESH,
        )

    def start_planes(i, carry):
        plane_copy(i).start()
        return carry

    lax.fori_loop(1, nj, start_planes, 0)

    for e in range(3, 9):
        asked_z(e).wait_recv()
    rreq_in = pltpu.make_async_copy(req_z, rreq_s, loc_sem.at[2])
    rreq_in.start()
    rreq_in.wait()

    def owner_of(e):
        return y * nz + (z + nz + serves[e][1]) % nz

    def brick(s, e, dy):
        d = ((y + dy) % ny) * nz + (z + nz + serves[e][0]) % nz
        return pltpu.make_async_remote_copy(
            src_ref=sendb.at[s, pl.ds((e * ny + dy) * cap, cap)],
            dst_ref=recvb[s].at[pl.ds(owner_of(e) * cap, cap)],
            send_sem=bsend_sem.at[s, e * ny + dy], recv_sem=brecv_sem.at[s, owner_of(e)],
            device_id=(sj, d), device_id_type=MESH,
        )

    def brick_from(s, d):
        return pltpu.make_async_remote_copy(
            src_ref=sendb.at[s, pl.ds(0, cap)], dst_ref=recvb[s].at[pl.ds(d * cap, cap)],
            send_sem=bsend_sem.at[s, 0], recv_sem=brecv_sem.at[s, d],
            device_id=(sj, sp), device_id_type=MESH,
        )

    def over_y(e, what):
        first, last, stride = serves[e][2]
        first = first + stride if serves[e][0] == 0 else first
        count = len(range(first, last, stride))

        def one(i, carry):
            what(first + i * stride)
            return carry

        if count:
            lax.fori_loop(0, count, one, 0)

    def wanted(s, e, dy, k):
        where = rreq_s[e, (y + dy) % ny, 0, s * cap + k]
        if serves[e][1] == 0:
            return img[s, where]
        return below[s][where] if serves[e][1] < 0 else above[s][where]

    for s in range(2):
        lent(s, 0).wait_recv()
        lent(s, 1).wait_recv()
        started = None
        for e in order[s]:

            def gather(dy, s=s, e=e):
                for k in range(cap):
                    sendb[s, (e * ny + dy) * cap + k] = wanted(s, e, dy, k)

            over_y(e, gather)
            if started is not None:
                over_y(started, lambda dy, s=s, e=started: brick(s, e, dy).start())
            started = e
        for e in range(3):
            for k in range(cap):
                recvb[s][owner_of(e) * cap + k] = wanted(s, e, 0, k)
        over_y(started, lambda dy, s=s, e=started: brick(s, e, dy).start())

    def wait_planes(i, carry):
        other = (sj + i) % nj
        pltpu.make_async_remote_copy(
            src_ref=tsend, dst_ref=trecv.at[other],
            send_sem=tsend_sem.at[0], recv_sem=trecv_sem.at[other],
            device_id=(sj, sp), device_id_type=MESH,
        ).wait_recv()
        return carry

    lax.fori_loop(1, nj, wait_planes, 0)
    trecv[sj] = tsend[...]
    for j in range(nj):
        for p in range(pd):
            cur0[pl.ds(j * pd + p, rows, stride=PLANE), :] = trecv[j, p]

    @pl.when(sp == 0)
    def _():
        halo[:, 0] = jnp.zeros_like(halo[:, 0])

    @pl.when(sp == ns - 1)
    def _():
        halo[:, 1] = jnp.zeros_like(halo[:, 1])

    wts_in.wait()
    vel_in.wait()
    slots_in.wait()

    lanes = lax.broadcasted_iota(I32, (8, LANES), 1)
    subs = lax.broadcasted_iota(I32, (8, LANES), 0)
    low = subs < 4
    y_top = subs % 4 == 3
    y_bot = subs % 4 == 0
    z_top = lanes == LANES - 1
    z_bot = lanes == 0

    def up_z(v):
        return jnp.where(z_top, 0.0, pltpu.roll(v, LANES - 1, 1))

    def down_z(v):
        return jnp.where(z_bot, 0.0, pltpu.roll(v, 1, 1))

    def up_y(v):
        return jnp.where(y_top, 0.0, pltpu.roll(v, 7, 0))

    def down_y(v):
        return jnp.where(y_bot, 0.0, pltpu.roll(v, 1, 0))

    def up_x(pair):
        a, b = [pltpu.roll(v, 4, 0) for v in pair]
        return [jnp.where(low, a, b), jnp.where(low, b, 0.0)]

    def pair_of(value):
        return [value[0:8], value[8:16]]

    def put(ref, index, pair):
        ref[index + (slice(0, 8),)] = pair[0]
        ref[index + (slice(8, 16),)] = pair[1]

    both = (0, 1)

    def arrivals(s):
        def far(n, carry):
            brick_from(s, ((y + 1 + n // nz) % ny) * nz + n % nz).wait_recv()
            return carry

        def near(n, carry):
            brick_from(s, y * nz + (z + n) % nz).wait_recv()
            return carry

        lax.fori_loop(0, (ny - 1) * nz, far, 0)
        lax.fori_loop(2, nz - 1, near, 0)

    def warp_blocks(s, start, stop):
        count = cnt_ref[0, s]
        first = count // 2
        last = rows - (count - first)

        def warp_tile(t):
            b00 = pair_of(recvb[s][slot_s[s, 0, t]].astype(F32))
            wx, wy, wz = [pair_of(wts[a, s, t].astype(F32)) for a in range(3)]
            live = jnp.where((t < first) | (t >= last), 1.0, 0.0).astype(F32)
            d00 = [up_z(v) - v for v in b00]
            b01, d01 = [up_y(v) for v in b00], [up_y(v) for v in d00]
            b10, d10 = up_x(b00), up_x(d00)
            b11, d11 = up_x(b01), up_x(d01)
            w = []
            for i in both:
                l00 = b00[i] + wz[i] * d00[i]
                l01 = b01[i] + wz[i] * d01[i]
                l10 = b10[i] + wz[i] * d10[i]
                l11 = b11[i] + wz[i] * d11[i]
                m0 = l00 + wy[i] * (l01 - l00)
                m1 = l10 + wy[i] * (l11 - l10)
                w.append((m0 + wx[i] * (m1 - m0)) * live)
            h = [0.5 * v for v in w]
            ra, rb = [pltpu.roll(v, 4, 0) for v in h]
            mid = jnp.where(low, ra, rb)
            gx = [mid - jnp.where(low, 0.0, ra), jnp.where(low, rb, 0.0) - mid]
            gy = [up_y(v) - down_y(v) for v in h]
            gz = [up_z(v) - down_z(v) for v in h]
            here = pl.multiple_of(t * PLANE, PLANE)
            now = pair_of(cur0[pl.ds(here, PLANE), :])
            fx0, fy0, fz0 = [pair_of(f[a, s, t]) for a in range(3)]
            qq, rr = [], []
            for i in both:
                sq = gx[i] * gx[i] + gy[i] * gy[i] + gz[i] * gz[i]
                inverse = 1.0 / (16.0 * sq + 4.0)
                pred = w[i] + (gx[i] * fx0[i] + gy[i] * fy0[i]) + gz[i] * fz0[i]
                qq.append(inverse)
                rr.append((pred - now[i]) * inverse)
            put(warp, (s, t), w)
            put(g, (0, s, t), gx)
            put(g, (1, s, t), gy)
            put(g, (2, s, t), gz)
            put(q, (s, t), qq)
            put(r, (s, t), rr)

        def warp_block(b, carry):
            for n in range(warp_step):
                warp_tile(b * warp_step + n)
            return carry

        lax.fori_loop(start, stop, warp_block, 0)

    def first_ratio(s, t):
        return pair_of(r[s, t])

    def second_ratio(s, t):
        here = pl.multiple_of(t * PLANE, PLANE)
        now = pair_of(cur1[pl.ds(here, PLANE), :])
        p1 = pair_of(pr[s, t])
        qq = pair_of(q[s, t])
        return [(p1[i] - now[i]) * qq[i] for i in both]

    def edge_copy(it, side, s):
        d = sp - 1 if side == 0 else sp + 1
        return pltpu.make_async_remote_copy(
            src_ref=edge.at[it, side, s], dst_ref=halo.at[it, 1 - side, s],
            send_sem=hsend_sem.at[it, side, s], recv_sem=hrecv_sem.at[it, 1 - side, s],
            device_id=(sj, d), device_id_type=MESH,
        )

    def halo_in(it, side, s):
        return pltpu.make_async_remote_copy(
            src_ref=edge.at[it, side, s], dst_ref=halo.at[it, side, s],
            send_sem=hsend_sem.at[it, side, s], recv_sem=hrecv_sem.at[it, side, s],
            device_id=(sj, sp), device_id_type=MESH,
        )

    def inside(side):
        return sp > 0 if side == 0 else sp < ns - 1

    def update(it, s, t):
        rr = first_ratio(s, t) if it == 0 else second_ratio(s, t)
        out = []
        for a in range(3):
            gg = pair_of(g[a, s, t])
            out += [gg[0] * rr[0], gg[1] * rr[1]]
        return out

    def send_edge(it, side, s):
        u = update(it, s, 0 if side == 0 else rows - 1)
        for a in range(3):
            put(edge, (it, side, s, a), u[2 * a : 2 * a + 2])

        @pl.when(inside(side))
        def _():
            edge_copy(it, side, s).start()

    def wait_halo(it, side, s):
        @pl.when(inside(side))
        def _():
            halo_in(it, side, s).wait_recv()

    def advance(it, s, t, v):
        new = []
        for a in range(3):
            old = pair_of(f[a, s, t])
            out = []
            for i in both:
                value = v[2 * a + i]
                two = value + down_z(value)
                out.append(old[i] - (two + jnp.where(z_top, value, pltpu.roll(two, LANES - 1, 1))))
            put(f, (a, s, t), out)
            new.append(out)
        w = pair_of(warp[s, t])
        gg = [pair_of(g[a, s, t]) for a in range(3)]
        pred = [
            w[i] + (gg[0][i] * new[0][i] + gg[1][i] * new[1][i]) + gg[2][i] * new[2][i]
            for i in both
        ]
        if it == 0:
            put(pr, (s, t), pred)
        here = pl.multiple_of(t * PLANE, PLANE)
        if s == 0:
            total[pl.ds(here, 8), :] = pred[0]
            total[pl.ds(here + 8, 8), :] = pred[1]
        else:
            total[pl.ds(here, 8), :] = total[pl.ds(here, 8), :] + pred[0]
            total[pl.ds(here + 8, 8), :] = total[pl.ds(here + 8, 8), :] + pred[1]

    def add(p, o):
        return [a + b for a, b in zip(p, o)]

    def run(it, s, start, low_row, high_row):
        u = update(it, s, start)
        two = add(low_row or update(it, s, start - 1), u)
        for n in range(step):
            at_end = n == step - 1
            after = high_row if at_end and high_row else update(it, s, start + n + 1)
            ahead = add(u, after)
            advance(it, s, start + n, add(two, ahead))
            u, two = after, ahead

    def smooth(it, s, start, stop):
        def inner(b, carry):
            run(it, s, b * step, None, None)
            return carry

        lax.fori_loop(start, stop, inner, 0)

    def smooth_edge(it, side, s):
        far = []
        for a in range(3):
            far += pair_of(halo[it, side, s, a])
        if side == 0:
            run(it, s, 0, far, None)
        else:
            run(it, s, rows - step, None, far)

    def chip(i):
        return (x + i) % nx

    quarter = rows // 4 * PLANE
    block = rows // (2 * nj) * PLANE
    scale = 1.0 / (2.0 * nj)

    def mine(k):
        return (2 * k + c) * quarter

    def other(k):
        return (2 * k + 1 - c) * quarter

    def to_mate(k):
        return pltpu.make_async_remote_copy(
            src_ref=total.at[pl.ds(other(k), quarter)], dst_ref=crecv.at[k],
            send_sem=csend_sem.at[k], recv_sem=crecv_sem.at[k],
            device_id=(mate, sp), device_id_type=MESH,
        )

    def across(k, i):
        return pltpu.make_async_remote_copy(
            src_ref=xsend.at[k, pl.ds(chip(i) * block, block)], dst_ref=xrecv.at[k, x],
            send_sem=xsend_sem.at[k, i], recv_sem=xrecv_sem.at[k, x],
            device_id=(chip(i) * 2 + c, sp), device_id_type=MESH,
        )

    def spread(k, i):
        return pltpu.make_async_remote_copy(
            src_ref=part.at[k], dst_ref=cur1.at[pl.ds(mine(k) + x * block, block)],
            send_sem=gsend_sem.at[k, i], recv_sem=grecv_sem.at[k, x],
            device_id=(chip(i) * 2 + c, sp), device_id_type=MESH,
        )

    def spread_mate(k, i):
        where = mine(k) + chip(i) * block
        return pltpu.make_async_remote_copy(
            src_ref=part.at[k] if i == 0 else cur1.at[pl.ds(where, block)],
            dst_ref=cur1.at[pl.ds(where, block)],
            send_sem=asend_sem.at[k, i], recv_sem=arecv_sem.at[k, i],
            device_id=(mate, sp), device_id_type=MESH,
        )

    def mean_pair(k):
        to_mate(k).wait_recv()
        xsend[k] = total[pl.ds(mine(k), quarter), :] + crecv[k]
        for i in range(1, nx):
            across(k, i).start()

    def mean_sum(k):
        acc = xsend[k, pl.ds(x * block, block), :]
        for i in range(1, nx):
            pltpu.make_async_remote_copy(
                src_ref=part.at[k], dst_ref=xrecv.at[k, chip(i)],
                send_sem=xsend_sem.at[k, i], recv_sem=xrecv_sem.at[k, chip(i)],
                device_id=(sj, sp), device_id_type=MESH,
            ).wait_recv()
            acc = acc + xrecv[k, chip(i)]
        part[k] = acc * scale
        for i in range(1, nx):
            spread(k, i).start()
        spread_mate(k, 0).start()
        cur1[pl.ds(mine(k) + x * block, block), :] = acc * scale

    def mean_pass(k):
        for i in range(1, nx):
            where = mine(k) + chip(i) * block
            pltpu.make_async_remote_copy(
                src_ref=part.at[k], dst_ref=cur1.at[pl.ds(where, block)],
                send_sem=gsend_sem.at[k, i], recv_sem=grecv_sem.at[k, chip(i)],
                device_id=(sj, sp), device_id_type=MESH,
            ).wait_recv()
            spread_mate(k, i).start()

    def mean_done(k):
        for i in range(nx):
            where = other(k) + chip(i) * block
            pltpu.make_async_remote_copy(
                src_ref=part.at[k], dst_ref=cur1.at[pl.ds(where, block)],
                send_sem=asend_sem.at[k, i], recv_sem=arecv_sem.at[k, i],
                device_id=(sj, sp), device_id_type=MESH,
            ).wait_recv()

    nb = rows // step
    nw = rows // warp_step
    mid = nb // 2

    arrivals(0)
    warp_blocks(0, 0, nw)
    send_edge(0, 0, 0)
    send_edge(0, 1, 0)
    smooth(0, 0, 1, nb - 1)
    arrivals(1)
    warp_blocks(1, nw - 1, nw)
    warp_blocks(1, 0, 1)
    send_edge(0, 0, 1)
    send_edge(0, 1, 1)
    warp_blocks(1, 1, nw - 1)
    smooth(0, 1, 1, mid)
    for s in range(2):
        wait_halo(0, 0, s)
        smooth_edge(0, 0, s)
    to_mate(0).start()
    smooth(0, 1, mid, nb - 1)
    mean_pair(0)
    for s in range(2):
        wait_halo(0, 1, s)
        smooth_edge(0, 1, s)
    to_mate(1).start()
    mean_pair(1)
    for k in range(2):
        mean_sum(k)
    for k in range(2):
        mean_pass(k)
    for k in range(2):
        to_mate(k).wait_send()

    mean_done(0)
    for s in range(2):
        send_edge(1, 0, s)
    for s in range(2):
        smooth(1, s, 1, mid - 1)
    mean_done(1)
    for s in range(2):
        send_edge(1, 1, s)
    for s in range(2):
        smooth(1, s, mid - 1, nb - 1)

    def sort_planes(b):
        base = b * step * PLANE
        for cc in range(2):
            for xx in range(nx):
                for p in range(pd):
                    plane = (2 * xx + cc) * pd + p
                    fsend[b, cc, xx, p] = total[pl.ds(base + plane, step, stride=PLANE), :]

    inner_blocks, ends = pl.ds(1, nb - 2), (pl.ds(0, 1), pl.ds(nb - 1, 1))
    pieces = (inner_blocks,) + ends

    def planes_to_mate(n):
        return pltpu.make_async_remote_copy(
            src_ref=fsend.at[pieces[n], 1 - c], dst_ref=frecv.at[pieces[n]],
            send_sem=fsend_sem.at[n], recv_sem=frecv_sem.at[n],
            device_id=(mate, sp), device_id_type=MESH,
        )

    def planes_across(n, i):
        return pltpu.make_async_remote_copy(
            src_ref=fx.at[chip(i), pieces[n]], dst_ref=fxrecv.at[x, pieces[n]],
            send_sem=ysend_sem.at[n, i], recv_sem=yrecv_sem.at[n, x],
            device_id=(chip(i) * 2 + c, sp), device_id_type=MESH,
        )

    def planes_pair(n, blocks):
        planes_to_mate(n).wait_recv()
        for b in blocks:
            for xx in range(nx):
                fx[xx, b] = fsend[b, c, xx] + frecv[b, xx]
        for i in range(1, nx):
            planes_across(n, i).start()

    def planes_sum(n, blocks):
        for i in range(1, nx):
            pltpu.make_async_remote_copy(
                src_ref=fxrecv.at[0, pieces[n]], dst_ref=fxrecv.at[chip(i), pieces[n]],
                send_sem=ysend_sem.at[n, i], recv_sem=yrecv_sem.at[n, chip(i)],
                device_id=(sj, sp), device_id_type=MESH,
            ).wait_recv()
        for b in blocks:
            acc = fx[x, b]
            for i in range(1, nx):
                acc = acc + fxrecv[chip(i), b]
            for p in range(pd):
                tout_ref[pl.ds(b * step * pd + p, step, stride=pd), :] = acc[p] * scale

    for b in range(1, nb - 1):
        sort_planes(b)
    planes_to_mate(0).start()
    for side in range(2):
        for s in range(2):
            wait_halo(1, side, s)
            smooth_edge(1, side, s)
        sort_planes(0 if side == 0 else nb - 1)
        planes_to_mate(1 + side).start()
        if side == 0:
            planes_pair(0, range(1, nb - 1))
    planes_pair(1, (0,))
    planes_pair(2, (nb - 1,))
    planes_sum(0, range(1, nb - 1))
    planes_sum(1, (0,))
    planes_sum(2, (nb - 1,))

    for i in range(1, ny):
        ask_y(i).wait_send()
    for e in range(3, 9):
        ask_z(e).wait_send()
    for s in range(2):
        lend(s, 0).wait_send()
        lend(s, 1).wait_send()
        for e in order[s]:
            over_y(e, lambda dy, s=s, e=e: brick(s, e, dy).wait_send())

    def sent_planes(i, carry):
        plane_copy(i).wait_send()
        return carry

    lax.fori_loop(1, nj, sent_planes, 0)
    for side in range(2):

        @pl.when(inside(side))
        def _():
            for it in range(2):
                for s in range(2):
                    edge_copy(it, side, s).wait_send()

    for k in range(2):
        for i in range(nx):
            spread_mate(k, i).wait_send()
        for i in range(1, nx):
            across(k, i).wait_send()
            spread(k, i).wait_send()
    for n in range(3):
        planes_to_mate(n).wait_send()
        for i in range(1, nx):
            planes_across(n, i).wait_send()


def body(nj, ny, nz, images, velocity, weights, template, owners, local_rows, tile_counts):
    ns = ny * nz
    nx = nj // 2
    rows = images.shape[1]
    pd = template.shape[1]
    cap = 2 * rows // ns
    slots = ns * cap
    brick = (PLANE, LANES)
    piece = rows // (2 * nj) * PLANE
    step = max(2, rows // 8)
    nb = rows // step
    vmem = pl.BlockSpec(memory_space=pltpu.VMEM)
    smem = pl.BlockSpec(memory_space=pltpu.SMEM)
    away = pl.BlockSpec(memory_space=pltpu.HBM)
    bf16 = jnp.bfloat16
    dma = pltpu.SemaphoreType.DMA
    field, planes = pl.pallas_call(
        functools.partial(kernel, nj, ny, nz, rows, cap),
        out_shape=(
            pltpu.VMEM(velocity.shape, F32),
            jax.ShapeDtypeStruct((rows * pd, LANES), F32),
        ),
        in_specs=[away, away, away, vmem, vmem, vmem, smem],
        out_specs=(vmem, vmem),
        scratch_shapes=[
            pltpu.VMEM((2, rows) + brick, bf16),
            pltpu.VMEM((rows,) + brick, bf16),
            pltpu.VMEM((rows,) + brick, bf16),
            pltpu.VMEM((rows,) + brick, bf16),
            pltpu.VMEM((rows,) + brick, bf16),
            pltpu.VMEM((3, 2, rows) + brick, bf16),
            pltpu.VMEM((2, 9 * ny * cap) + brick, bf16),
            pltpu.VMEM((slots,) + brick, bf16),
            pltpu.VMEM((slots,) + brick, bf16),
            pltpu.VMEM((2, rows) + brick, F32),
            pltpu.VMEM((3, 2, rows) + brick, F32),
            pltpu.VMEM((2, rows) + brick, F32),
            pltpu.VMEM((2, rows) + brick, F32),
            pltpu.VMEM((2, rows) + brick, F32),
            pltpu.VMEM((rows * PLANE, LANES), F32),
            pltpu.VMEM((rows * PLANE, LANES), F32),
            pltpu.VMEM((rows * PLANE, LANES), F32),
            pltpu.VMEM((pd, rows, LANES), F32),
            pltpu.VMEM((nj, pd, rows, LANES), F32),
            pltpu.VMEM((ny, nz, 1, LANES), I32),
            pltpu.VMEM((ny, nz, 1, LANES), I32),
            pltpu.VMEM((9, ny, 1, LANES), I32),
            pltpu.VMEM((2, 1, LANES), I32),
            pltpu.SMEM((9, ny, 1, LANES), I32),
            pltpu.SMEM((2, 1, LANES), I32),
            pltpu.VMEM((2, 2, 2, 3) + brick, F32),
            pltpu.VMEM((2, 2, 2, 3) + brick, F32),
            pltpu.VMEM((2, piece, LANES), F32),
            pltpu.VMEM((2, rows // 4 * PLANE, LANES), F32),
            pltpu.VMEM((2, rows // 4 * PLANE, LANES), F32),
            pltpu.VMEM((2, nx, piece, LANES), F32),
            pltpu.VMEM((nb, 2, nx, pd, step, LANES), F32),
            pltpu.VMEM((nb, nx, pd, step, LANES), F32),
            pltpu.VMEM((nx, nb, pd, step, LANES), F32),
            pltpu.VMEM((nx, nb, pd, step, LANES), F32),
            dma((3,)), dma((nj,)), dma((nj,)), dma((2, 9)), dma((2, 9)), dma((4,)),
            dma((2, 2)), dma((2, 2)), dma((2, 9 * ny)), dma((2, ns)), dma((2, 2, 2)), dma((2, 2, 2)),
            dma((2,)), dma((2,)), dma((2, nx)), dma((2, nx)), dma((2, nx)), dma((2, nx)),
            dma((2, nx)), dma((2, nx)), dma((3,)), dma((3,)), dma((3, nx)), dma((3, nx)),
        ],
        compiler_params=pltpu.CompilerParams(
            collective_id=0, has_side_effects=True, vmem_limit_bytes=62200 * 1024
        ),
        name="demons",
    )(
        images, velocity, weights, template.reshape(rows * pd, LANES),
        jnp.swapaxes(owners, 1, 2), local_rows, tile_counts.T,
    )
    return field, planes.reshape(template.shape)


def solution(mesh):
    nj, ns = mesh.shape["subj"], mesh.shape["space"]
    nz = 8 if ns % 8 == 0 else 2
    in_specs = (
        P("subj", "space", None, None),
        P(None, "subj", "space", None, None),
        P(None, "subj", "space", None, None),
        P("space", "subj", None),
        P("subj", "space", None),
        P("subj", "space"),
        P("subj", "space"),
    )
    out_specs = (P(None, "subj", "space", None, None), P("space", "subj", None))
    return jax.shard_map(
        functools.partial(body, nj, ns // nz, nz),
        mesh=mesh, in_specs=in_specs, out_specs=out_specs, check_vma=False,
    )
```

```python
import functools

import jax
import jax.numpy as jnp
from jax import lax
from jax.experimental import pallas as pl
from jax.experimental.pallas import tpu as pltpu
from jax.sharding import PartitionSpec as P

MESH = pl.DeviceIdType.MESH
F32 = jnp.float32
I32 = jnp.int32
PLANE = 16
LANES = 128


def kernel(
    nj, ny, nz, rows, cap,
    img_h, vel_h, wts_h, tin_ref, own_ref, loc_ref, cnt_ref,
    f, tout_ref,
    img, below0, below1, above0, above1, wts, sendb, recvb0, recvb1, warp, g, q, r, pr, cur0, cur1, total,
    tsend, trecv, req, req_y, req_z, slot_v, rreq_s, slot_s, edge, halo,
    part, crecv, xsend, xrecv, fsend, frecv, fx, fxrecv,
    in_sem, tsend_sem, trecv_sem, qsend_sem, qrecv_sem, loc_sem,
    lsend_sem, lrecv_sem, bsend_sem, brecv_sem, hsend_sem, hrecv_sem,
    csend_sem, crecv_sem, xsend_sem, xrecv_sem, gsend_sem, grecv_sem,
    asend_sem, arecv_sem, fsend_sem, frecv_sem, ysend_sem, yrecv_sem,
):
    ns = ny * nz
    nx = nj // 2
    pd = PLANE // nj
    sj = lax.axis_index("subj")
    sp = lax.axis_index("space")
    x, c = sj // 2, sj % 2
    y, z = sp // nz, sp % nz
    mate = x * 2 + (1 - c)
    recvb = (recvb0, recvb1)
    warp_step = 8 if rows >= 32 else 2
    step = max(2, rows // 8)

    every, even, odd = (0, ny, 1), (0, ny, 2), (1, ny, 2)
    serves = (
        (0, 0, every), (0, -1, every), (0, 1, every),
        (1, -1, every), (2, -1, every), (3, -1, even),
        (-1, 1, every), (-2, 1, every), (-3, 1, odd),
    )
    order = ((1, 2, 0, 5, 8, 4, 7, 3, 6), (5, 8, 4, 7, 3, 6, 1, 2, 0))

    img_in = pltpu.make_async_copy(img_h, img, in_sem.at[0])
    img_in.start()
    wts_in = pltpu.make_async_copy(wts_h, wts, in_sem.at[1])
    wts_in.start()
    vel_in = pltpu.make_async_copy(vel_h, f, in_sem.at[2])
    vel_in.start()

    barrier = pltpu.get_barrier_semaphore()

    def along_y(i):
        return ((y + i) % ny) * nz + z

    def along_z(i):
        return y * nz + (z + nz + i) % nz

    for i in range(1, ny):
        pl.semaphore_signal(barrier, inc=1, device_id=(sj, along_y(i)), device_id_type=MESH)
    for e in range(3, 9):
        pl.semaphore_signal(barrier, inc=1, device_id=(sj, along_z(serves[e][0])), device_id_type=MESH)

    def greet_subj(i, carry):
        pl.semaphore_signal(barrier, inc=1, device_id=((sj + i) % nj, sp), device_id_type=MESH)
        return carry

    lax.fori_loop(1, nj, greet_subj, 0)

    for p in range(pd):
        tsend[p] = tin_ref[pl.ds(p, rows, stride=pd), :]

    i0 = lax.broadcasted_iota(I32, (rows, rows), 0)
    i1 = lax.broadcasted_iota(I32, (rows, rows), 1)
    who = lax.broadcasted_iota(I32, (ns, rows), 0)
    lane = lax.broadcasted_iota(I32, (ns, LANES), 1)
    asked = jnp.zeros((ns, LANES), I32)
    slot_v[...] = jnp.zeros_like(slot_v)
    for s in range(2):
        count = cnt_ref[0, s]
        first = count // 2
        last = rows - (count - first)
        row = own_ref[s]
        col = jnp.sum(jnp.where(i0 == i1, row, 0), axis=1, keepdims=True)
        alive0 = (i0 < first) | (i0 >= last)
        hit = (col == row) & (i0 < i1) & alive0
        before = jnp.sum(jnp.where(hit, 1, 0), axis=0, keepdims=True)
        t1 = i1[0:1, :]
        alive1 = (t1 < first) | (t1 >= last)
        slot = jnp.where(alive1, row * cap + before, 0)
        slot_v[s, :, 0:rows] = slot
        place = jnp.where(alive1, before, cap)
        for k in range(cap):
            mine = (row == who) & (place == k)
            column = jnp.sum(jnp.where(mine, loc_ref[s : s + 1, :], 0), axis=1, keepdims=True)
            asked = asked + jnp.where(lane == s * cap + k, column, 0)
    for d in range(ns):
        req[d // nz, d % nz] = asked[d : d + 1, :]
    slots_in = pltpu.make_async_copy(slot_v, slot_s, loc_sem.at[0])
    slots_in.start()

    pl.semaphore_wait(barrier, ny - 1 + 6 + nj - 1)

    def ask_y(i):
        return pltpu.make_async_remote_copy(
            src_ref=req.at[(y + i) % ny], dst_ref=req_y.at[y],
            send_sem=qsend_sem.at[0, i], recv_sem=qrecv_sem.at[0, y],
            device_id=(sj, along_y(i)), device_id_type=MESH,
        )

    def asked_y(i):
        return pltpu.make_async_remote_copy(
            src_ref=req.at[0], dst_ref=req_y.at[(y + i) % ny],
            send_sem=qsend_sem.at[0, i], recv_sem=qrecv_sem.at[0, (y + i) % ny],
            device_id=(sj, sp), device_id_type=MESH,
        )

    def ask_z(e):
        back, image, _ = serves[e]
        return pltpu.make_async_remote_copy(
            src_ref=req_y.at[:, (z + nz - back + image) % nz], dst_ref=req_z.at[e],
            send_sem=qsend_sem.at[1, e], recv_sem=qrecv_sem.at[1, e],
            device_id=(sj, along_z(-back)), device_id_type=MESH,
        )

    def asked_z(e):
        return pltpu.make_async_remote_copy(
            src_ref=req_y.at[:, 0], dst_ref=req_z.at[e],
            send_sem=qsend_sem.at[1, e], recv_sem=qrecv_sem.at[1, e],
            device_id=(sj, sp), device_id_type=MESH,
        )

    below, above = (below0, below1), (above0, above1)

    def lend(s, side):
        return pltpu.make_async_remote_copy(
            src_ref=img.at[s], dst_ref=below[s] if side == 0 else above[s],
            send_sem=lsend_sem.at[s, side], recv_sem=lrecv_sem.at[s, side],
            device_id=(sj, along_z(1 if side == 0 else -1)), device_id_type=MESH,
        )

    def lent(s, side):
        return pltpu.make_async_remote_copy(
            src_ref=img.at[s], dst_ref=below[s] if side == 0 else above[s],
            send_sem=lsend_sem.at[s, side], recv_sem=lrecv_sem.at[s, side],
            device_id=(sj, sp), device_id_type=MESH,
        )

    for i in range(1, ny):
        ask_y(i).start()
    img_in.wait()
    lend(0, 0).start()
    lend(0, 1).start()
    req_y[y] = req[y]
    for i in range(1, ny):
        asked_y(i).wait_recv()
    for e in (5, 8, 4, 7, 3, 6):
        ask_z(e).start()
    lend(1, 0).start()
    lend(1, 1).start()
    for e in range(3):
        for n in range(ny):
            req_z[e, n] = req_y[n, (z + nz + serves[e][1]) % nz]

    def plane_copy(i):
        return pltpu.make_async_remote_copy(
            src_ref=tsend, dst_ref=trecv.at[sj],
            send_sem=tsend_sem.at[i], recv_sem=trecv_sem.at[sj],
            device_id=((sj + i) % nj, sp), device_id_type=MESH,
        )

    def start_planes(i, carry):
        plane_copy(i).start()
        return carry

    lax.fori_loop(1, nj, start_planes, 0)

    for e in range(3, 9):
        asked_z(e).wait_recv()
    rreq_in = pltpu.make_async_copy(req_z, rreq_s, loc_sem.at[2])
    rreq_in.start()
    rreq_in.wait()

    def owner_of(e):
        return y * nz + (z + nz + serves[e][1]) % nz

    def brick(s, e, dy):
        d = ((y + dy) % ny) * nz + (z + nz + serves[e][0]) % nz
        return pltpu.make_async_remote_copy(
            src_ref=sendb.at[s, pl.ds((e * ny + dy) * cap, cap)],
            dst_ref=recvb[s].at[pl.ds(owner_of(e) * cap, cap)],
            send_sem=bsend_sem.at[s, e * ny + dy], recv_sem=brecv_sem.at[s, owner_of(e)],
            device_id=(sj, d), device_id_type=MESH,
        )

    def brick_from(s, d):
        return pltpu.make_async_remote_copy(
            src_ref=sendb.at[s, pl.ds(0, cap)], dst_ref=recvb[s].at[pl.ds(d * cap, cap)],
            send_sem=bsend_sem.at[s, 0], recv_sem=brecv_sem.at[s, d],
            device_id=(sj, sp), device_id_type=MESH,
        )

    def over_y(e, what):
        first, last, stride = serves[e][2]
        first = first + stride if serves[e][0] == 0 else first
        count = len(range(first, last, stride))

        def one(i, carry):
            what(first + i * stride)
            return carry

        if count:
            lax.fori_loop(0, count, one, 0)

    def wanted(s, e, dy, k):
        where = rreq_s[e, (y + dy) % ny, 0, s * cap + k]
        if serves[e][1] == 0:
            return img[s, where]
        return below[s][where] if serves[e][1] < 0 else above[s][where]

    for s in range(2):
        lent(s, 0).wait_recv()
        lent(s, 1).wait_recv()
        started = None
        for e in order[s]:

            def gather(dy, s=s, e=e):
                for k in range(cap):
                    sendb[s, (e * ny + dy) * cap + k] = wanted(s, e, dy, k)

            over_y(e, gather)
            if started is not None:
                over_y(started, lambda dy, s=s, e=started: brick(s, e, dy).start())
            started = e
        for e in range(3):
            for k in range(cap):
                recvb[s][owner_of(e) * cap + k] = wanted(s, e, 0, k)
        over_y(started, lambda dy, s=s, e=started: brick(s, e, dy).start())

    def wait_planes(i, carry):
        other = (sj + i) % nj
        pltpu.make_async_remote_copy(
            src_ref=tsend, dst_ref=trecv.at[other],
            send_sem=tsend_sem.at[0], recv_sem=trecv_sem.at[other],
            device_id=(sj, sp), device_id_type=MESH,
        ).wait_recv()
        return carry

    lax.fori_loop(1, nj, wait_planes, 0)
    trecv[sj] = tsend[...]
    for j in range(nj):
        for p in range(pd):
            cur0[pl.ds(j * pd + p, rows, stride=PLANE), :] = trecv[j, p]

    @pl.when(sp == 0)
    def _():
        halo[:, 0] = jnp.zeros_like(halo[:, 0])

    @pl.when(sp == ns - 1)
    def _():
        halo[:, 1] = jnp.zeros_like(halo[:, 1])

    wts_in.wait()
    vel_in.wait()
    slots_in.wait()

    lanes = lax.broadcasted_iota(I32, (8, LANES), 1)
    subs = lax.broadcasted_iota(I32, (8, LANES), 0)
    low = subs < 4
    y_top = subs % 4 == 3
    y_bot = subs % 4 == 0
    z_top = lanes == LANES - 1
    z_bot = lanes == 0

    def up_z(v):
        return jnp.where(z_top, 0.0, pltpu.roll(v, LANES - 1, 1))

    def down_z(v):
        return jnp.where(z_bot, 0.0, pltpu.roll(v, 1, 1))

    def up_y(v):
        return jnp.where(y_top, 0.0, pltpu.roll(v, 7, 0))

    def down_y(v):
        return jnp.where(y_bot, 0.0, pltpu.roll(v, 1, 0))

    def up_x(pair):
        a, b = [pltpu.roll(v, 4, 0) for v in pair]
        return [jnp.where(low, a, b), jnp.where(low, b, 0.0)]

    def pair_of(value):
        return [value[0:8], value[8:16]]

    def put(ref, index, pair):
        ref[index + (slice(0, 8),)] = pair[0]
        ref[index + (slice(8, 16),)] = pair[1]

    both = (0, 1)

    def arrivals(s):
        def far(n, carry):
            brick_from(s, ((y + 1 + n // nz) % ny) * nz + n % nz).wait_recv()
            return carry

        def near(n, carry):
            brick_from(s, y * nz + (z + n) % nz).wait_recv()
            return carry

        lax.fori_loop(0, (ny - 1) * nz, far, 0)
        lax.fori_loop(2, nz - 1, near, 0)

    def warp_blocks(s, start, stop):
        count = cnt_ref[0, s]
        first = count // 2
        last = rows - (count - first)

        def warp_tile(t):
            b00 = pair_of(recvb[s][slot_s[s, 0, t]].astype(F32))
            wx, wy, wz = [pair_of(wts[a, s, t].astype(F32)) for a in range(3)]
            live = jnp.where((t < first) | (t >= last), 1.0, 0.0).astype(F32)
            d00 = [up_z(v) - v for v in b00]
            b01, d01 = [up_y(v) for v in b00], [up_y(v) for v in d00]
            b10, d10 = up_x(b00), up_x(d00)
            b11, d11 = up_x(b01), up_x(d01)
            w = []
            for i in both:
                l00 = b00[i] + wz[i] * d00[i]
                l01 = b01[i] + wz[i] * d01[i]
                l10 = b10[i] + wz[i] * d10[i]
                l11 = b11[i] + wz[i] * d11[i]
                m0 = l00 + wy[i] * (l01 - l00)
                m1 = l10 + wy[i] * (l11 - l10)
                w.append((m0 + wx[i] * (m1 - m0)) * live)
            h = [0.5 * v for v in w]
            ra, rb = [pltpu.roll(v, 4, 0) for v in h]
            mid = jnp.where(low, ra, rb)
            gx = [mid - jnp.where(low, 0.0, ra), jnp.where(low, rb, 0.0) - mid]
            gy = [up_y(v) - down_y(v) for v in h]
            gz = [up_z(v) - down_z(v) for v in h]
            here = pl.multiple_of(t * PLANE, PLANE)
            now = pair_of(cur0[pl.ds(here, PLANE), :])
            fx0, fy0, fz0 = [pair_of(f[a, s, t]) for a in range(3)]
            qq, rr = [], []
            for i in both:
                sq = gx[i] * gx[i] + gy[i] * gy[i] + gz[i] * gz[i]
                inverse = 1.0 / (16.0 * sq + 4.0)
                pred = w[i] + (gx[i] * fx0[i] + gy[i] * fy0[i]) + gz[i] * fz0[i]
                qq.append(inverse)
                rr.append((pred - now[i]) * inverse)
            put(warp, (s, t), w)
            put(g, (0, s, t), gx)
            put(g, (1, s, t), gy)
            put(g, (2, s, t), gz)
            put(q, (s, t), qq)
            put(r, (s, t), rr)

        def warp_block(b, carry):
            for n in range(warp_step):
                warp_tile(b * warp_step + n)
            return carry

        lax.fori_loop(start, stop, warp_block, 0)

    def first_ratio(s, t):
        return pair_of(r[s, t])

    def second_ratio(s, t):
        here = pl.multiple_of(t * PLANE, PLANE)
        now = pair_of(cur1[pl.ds(here, PLANE), :])
        p1 = pair_of(pr[s, t])
        qq = pair_of(q[s, t])
        return [(p1[i] - now[i]) * qq[i] for i in both]

    def edge_copy(it, side, s):
        d = sp - 1 if side == 0 else sp + 1
        return pltpu.make_async_remote_copy(
            src_ref=edge.at[it, side, s], dst_ref=halo.at[it, 1 - side, s],
            send_sem=hsend_sem.at[it, side, s], recv_sem=hrecv_sem.at[it, 1 - side, s],
            device_id=(sj, d), device_id_type=MESH,
        )

    def halo_in(it, side, s):
        return pltpu.make_async_remote_copy(
            src_ref=edge.at[it, side, s], dst_ref=halo.at[it, side, s],
            send_sem=hsend_sem.at[it, side, s], recv_sem=hrecv_sem.at[it, side, s],
            device_id=(sj, sp), device_id_type=MESH,
        )

    def inside(side):
        return sp > 0 if side == 0 else sp < ns - 1

    def update(it, s, t):
        rr = first_ratio(s, t) if it == 0 else second_ratio(s, t)
        out = []
        for a in range(3):
            gg = pair_of(g[a, s, t])
            out += [gg[0] * rr[0], gg[1] * rr[1]]
        return out

    def send_edge(it, side, s):
        u = update(it, s, 0 if side == 0 else rows - 1)
        for a in range(3):
            put(edge, (it, side, s, a), u[2 * a : 2 * a + 2])

        @pl.when(inside(side))
        def _():
            edge_copy(it, side, s).start()

    def wait_halo(it, side, s):
        @pl.when(inside(side))
        def _():
            halo_in(it, side, s).wait_recv()

    def advance(it, s, t, v):
        new = []
        for a in range(3):
            old = pair_of(f[a, s, t])
            out = []
            for i in both:
                value = v[2 * a + i]
                two = value + down_z(value)
                out.append(old[i] - (two + jnp.where(z_top, value, pltpu.roll(two, LANES - 1, 1))))
            put(f, (a, s, t), out)
            new.append(out)
        w = pair_of(warp[s, t])
        gg = [pair_of(g[a, s, t]) for a in range(3)]
        pred = [
            w[i] + (gg[0][i] * new[0][i] + gg[1][i] * new[1][i]) + gg[2][i] * new[2][i]
            for i in both
        ]
        if it == 0:
            put(pr, (s, t), pred)
        here = pl.multiple_of(t * PLANE, PLANE)
        if s == 0:
            total[pl.ds(here, 8), :] = pred[0]
            total[pl.ds(here + 8, 8), :] = pred[1]
        else:
            total[pl.ds(here, 8), :] = total[pl.ds(here, 8), :] + pred[0]
            total[pl.ds(here + 8, 8), :] = total[pl.ds(here + 8, 8), :] + pred[1]

    def add(p, o):
        return [a + b for a, b in zip(p, o)]

    def run(it, s, start, low_row, high_row):
        u = update(it, s, start)
        two = add(low_row or update(it, s, start - 1), u)
        for n in range(step):
            at_end = n == step - 1
            after = high_row if at_end and high_row else update(it, s, start + n + 1)
            ahead = add(u, after)
            advance(it, s, start + n, add(two, ahead))
            u, two = after, ahead

    def smooth(it, s, start, stop):
        def inner(b, carry):
            run(it, s, b * step, None, None)
            return carry

        lax.fori_loop(start, stop, inner, 0)

    def smooth_edge(it, side, s):
        far = []
        for a in range(3):
            far += pair_of(halo[it, side, s, a])
        if side == 0:
            run(it, s, 0, far, None)
        else:
            run(it, s, rows - step, None, far)

    def chip(i):
        return (x + i) % nx

    quarter = rows // 4 * PLANE
    block = rows // (2 * nj) * PLANE
    scale = 1.0 / (2.0 * nj)

    def mine(k):
        return (2 * k + c) * quarter

    def other(k):
        return (2 * k + 1 - c) * quarter

    def to_mate(k):
        return pltpu.make_async_remote_copy(
            src_ref=total.at[pl.ds(other(k), quarter)], dst_ref=crecv.at[k],
            send_sem=csend_sem.at[k], recv_sem=crecv_sem.at[k],
            device_id=(mate, sp), device_id_type=MESH,
        )

    def across(k, i):
        return pltpu.make_async_remote_copy(
            src_ref=xsend.at[k, pl.ds(chip(i) * block, block)], dst_ref=xrecv.at[k, x],
            send_sem=xsend_sem.at[k, i], recv_sem=xrecv_sem.at[k, x],
            device_id=(chip(i) * 2 + c, sp), device_id_type=MESH,
        )

    def spread(k, i):
        return pltpu.make_async_remote_copy(
            src_ref=part.at[k], dst_ref=cur1.at[pl.ds(mine(k) + x * block, block)],
            send_sem=gsend_sem.at[k, i], recv_sem=grecv_sem.at[k, x],
            device_id=(chip(i) * 2 + c, sp), device_id_type=MESH,
        )

    def spread_mate(k, i):
        where = mine(k) + chip(i) * block
        return pltpu.make_async_remote_copy(
            src_ref=part.at[k] if i == 0 else cur1.at[pl.ds(where, block)],
            dst_ref=cur1.at[pl.ds(where, block)],
            send_sem=asend_sem.at[k, i], recv_sem=arecv_sem.at[k, i],
            device_id=(mate, sp), device_id_type=MESH,
        )

    def mean_pair(k):
        to_mate(k).wait_recv()
        xsend[k] = total[pl.ds(mine(k), quarter), :] + crecv[k]
        for i in range(1, nx):
            across(k, i).start()

    def mean_sum(k):
        acc = xsend[k, pl.ds(x * block, block), :]
        for i in range(1, nx):
            pltpu.make_async_remote_copy(
                src_ref=part.at[k], dst_ref=xrecv.at[k, chip(i)],
                send_sem=xsend_sem.at[k, i], recv_sem=xrecv_sem.at[k, chip(i)],
                device_id=(sj, sp), device_id_type=MESH,
            ).wait_recv()
            acc = acc + xrecv[k, chip(i)]
        part[k] = acc * scale
        for i in range(1, nx):
            spread(k, i).start()
        spread_mate(k, 0).start()
        cur1[pl.ds(mine(k) + x * block, block), :] = acc * scale

    def mean_pass(k):
        for i in range(1, nx):
            where = mine(k) + chip(i) * block
            pltpu.make_async_remote_copy(
                src_ref=part.at[k], dst_ref=cur1.at[pl.ds(where, block)],
                send_sem=gsend_sem.at[k, i], recv_sem=grecv_sem.at[k, chip(i)],
                device_id=(sj, sp), device_id_type=MESH,
            ).wait_recv()
            spread_mate(k, i).start()

    def mean_done(k):
        for i in range(nx):
            where = other(k) + chip(i) * block
            pltpu.make_async_remote_copy(
                src_ref=part.at[k], dst_ref=cur1.at[pl.ds(where, block)],
                send_sem=asend_sem.at[k, i], recv_sem=arecv_sem.at[k, i],
                device_id=(sj, sp), device_id_type=MESH,
            ).wait_recv()

    nb = rows // step
    nw = rows // warp_step
    mid = nb // 2

    arrivals(0)
    warp_blocks(0, 0, nw)
    send_edge(0, 0, 0)
    send_edge(0, 1, 0)
    smooth(0, 0, 1, nb - 1)
    arrivals(1)
    warp_blocks(1, nw - 1, nw)
    warp_blocks(1, 0, 1)
    send_edge(0, 0, 1)
    send_edge(0, 1, 1)
    warp_blocks(1, 1, nw - 1)
    smooth(0, 1, 1, mid)
    for s in range(2):
        wait_halo(0, 0, s)
        smooth_edge(0, 0, s)
    to_mate(0).start()
    smooth(0, 1, mid, nb - 1)
    mean_pair(0)
    for s in range(2):
        wait_halo(0, 1, s)
        smooth_edge(0, 1, s)
    to_mate(1).start()
    mean_pair(1)
    for k in range(2):
        mean_sum(k)
    for k in range(2):
        mean_pass(k)
    for k in range(2):
        to_mate(k).wait_send()

    mean_done(0)
    for s in range(2):
        send_edge(1, 0, s)
    for s in range(2):
        smooth(1, s, 1, mid - 1)
    mean_done(1)
    for s in range(2):
        send_edge(1, 1, s)
    for s in range(2):
        smooth(1, s, mid - 1, nb - 1)

    def sort_planes(b):
        base = b * step * PLANE
        for cc in range(2):
            for xx in range(nx):
                for p in range(pd):
                    plane = (2 * xx + cc) * pd + p
                    fsend[b, cc, xx, p] = total[pl.ds(base + plane, step, stride=PLANE), :]

    inner_blocks, ends = pl.ds(1, nb - 2), (pl.ds(0, 1), pl.ds(nb - 1, 1))
    pieces = (inner_blocks,) + ends

    def planes_to_mate(n):
        return pltpu.make_async_remote_copy(
            src_ref=fsend.at[pieces[n], 1 - c], dst_ref=frecv.at[pieces[n]],
            send_sem=fsend_sem.at[n], recv_sem=frecv_sem.at[n],
            device_id=(mate, sp), device_id_type=MESH,
        )

    def planes_across(n, i):
        return pltpu.make_async_remote_copy(
            src_ref=fx.at[chip(i), pieces[n]], dst_ref=fxrecv.at[x, pieces[n]],
            send_sem=ysend_sem.at[n, i], recv_sem=yrecv_sem.at[n, x],
            device_id=(chip(i) * 2 + c, sp), device_id_type=MESH,
        )

    def planes_pair(n, blocks):
        planes_to_mate(n).wait_recv()
        for b in blocks:
            for xx in range(nx):
                fx[xx, b] = fsend[b, c, xx] + frecv[b, xx]
        for i in range(1, nx):
            planes_across(n, i).start()

    def planes_sum(n, blocks):
        for i in range(1, nx):
            pltpu.make_async_remote_copy(
                src_ref=fxrecv.at[0, pieces[n]], dst_ref=fxrecv.at[chip(i), pieces[n]],
                send_sem=ysend_sem.at[n, i], recv_sem=yrecv_sem.at[n, chip(i)],
                device_id=(sj, sp), device_id_type=MESH,
            ).wait_recv()
        for b in blocks:
            acc = fx[x, b]
            for i in range(1, nx):
                acc = acc + fxrecv[chip(i), b]
            for p in range(pd):
                tout_ref[pl.ds(b * step * pd + p, step, stride=pd), :] = acc[p] * scale

    for b in range(1, nb - 1):
        sort_planes(b)
    planes_to_mate(0).start()
    for side in range(2):
        for s in range(2):
            wait_halo(1, side, s)
            smooth_edge(1, side, s)
        sort_planes(0 if side == 0 else nb - 1)
        planes_to_mate(1 + side).start()
        if side == 0:
            planes_pair(0, range(1, nb - 1))
    planes_pair(1, (0,))
    planes_pair(2, (nb - 1,))
    planes_sum(0, range(1, nb - 1))
    planes_sum(1, (0,))
    planes_sum(2, (nb - 1,))

    for i in range(1, ny):
        ask_y(i).wait_send()
    for e in range(3, 9):
        ask_z(e).wait_send()
    for s in range(2):
        lend(s, 0).wait_send()
        lend(s, 1).wait_send()
        for e in order[s]:
            over_y(e, lambda dy, s=s, e=e: brick(s, e, dy).wait_send())

    def sent_planes(i, carry):
        plane_copy(i).wait_send()
        return carry

    lax.fori_loop(1, nj, sent_planes, 0)
    for side in range(2):

        @pl.when(inside(side))
        def _():
            for it in range(2):
                for s in range(2):
                    edge_copy(it, side, s).wait_send()

    for k in range(2):
        for i in range(nx):
            spread_mate(k, i).wait_send()
        for i in range(1, nx):
            across(k, i).wait_send()
            spread(k, i).wait_send()
    for n in range(3):
        planes_to_mate(n).wait_send()
        for i in range(1, nx):
            planes_across(n, i).wait_send()


def body(nj, ny, nz, images, velocity, weights, template, owners, local_rows, tile_counts):
    ns = ny * nz
    nx = nj // 2
    rows = images.shape[1]
    pd = template.shape[1]
    cap = 2 * rows // ns
    slots = ns * cap
    brick = (PLANE, LANES)
    piece = rows // (2 * nj) * PLANE
    step = max(2, rows // 8)
    nb = rows // step
    vmem = pl.BlockSpec(memory_space=pltpu.VMEM)
    smem = pl.BlockSpec(memory_space=pltpu.SMEM)
    away = pl.BlockSpec(memory_space=pltpu.HBM)
    bf16 = jnp.bfloat16
    dma = pltpu.SemaphoreType.DMA
    field, planes = pl.pallas_call(
        functools.partial(kernel, nj, ny, nz, rows, cap),
        out_shape=(
            pltpu.VMEM(velocity.shape, F32),
            pltpu.VMEM((rows * pd, LANES), F32),
        ),
        in_specs=[away, away, away, vmem, vmem, vmem, smem],
        out_specs=(vmem, vmem),
        scratch_shapes=[
            pltpu.VMEM((2, rows) + brick, bf16),
            pltpu.VMEM((rows,) + brick, bf16),
            pltpu.VMEM((rows,) + brick, bf16),
            pltpu.VMEM((rows,) + brick, bf16),
            pltpu.VMEM((rows,) + brick, bf16),
            pltpu.VMEM((3, 2, rows) + brick, bf16),
            pltpu.VMEM((2, 9 * ny * cap) + brick, bf16),
            pltpu.VMEM((slots,) + brick, bf16),
            pltpu.VMEM((slots,) + brick, bf16),
            pltpu.VMEM((2, rows) + brick, F32),
            pltpu.VMEM((3, 2, rows) + brick, F32),
            pltpu.VMEM((2, rows) + brick, F32),
            pltpu.VMEM((2, rows) + brick, F32),
            pltpu.VMEM((2, rows) + brick, F32),
            pltpu.VMEM((rows * PLANE, LANES), F32),
            pltpu.VMEM((rows * PLANE, LANES), F32),
            pltpu.VMEM((rows * PLANE, LANES), F32),
            pltpu.VMEM((pd, rows, LANES), F32),
            pltpu.VMEM((nj, pd, rows, LANES), F32),
            pltpu.VMEM((ny, nz, 1, LANES), I32),
            pltpu.VMEM((ny, nz, 1, LANES), I32),
            pltpu.VMEM((9, ny, 1, LANES), I32),
            pltpu.VMEM((2, 1, LANES), I32),
            pltpu.SMEM((9, ny, 1, LANES), I32),
            pltpu.SMEM((2, 1, LANES), I32),
            pltpu.VMEM((2, 2, 2, 3) + brick, F32),
            pltpu.VMEM((2, 2, 2, 3) + brick, F32),
            pltpu.VMEM((2, piece, LANES), F32),
            pltpu.VMEM((2, rows // 4 * PLANE, LANES), F32),
            pltpu.VMEM((2, rows // 4 * PLANE, LANES), F32),
            pltpu.VMEM((2, nx, piece, LANES), F32),
            pltpu.VMEM((nb, 2, nx, pd, step, LANES), F32),
            pltpu.VMEM((nb, nx, pd, step, LANES), F32),
            pltpu.VMEM((nx, nb, pd, step, LANES), F32),
            pltpu.VMEM((nx, nb, pd, step, LANES), F32),
            dma((3,)), dma((nj,)), dma((nj,)), dma((2, 9)), dma((2, 9)), dma((4,)),
            dma((2, 2)), dma((2, 2)), dma((2, 9 * ny)), dma((2, ns)), dma((2, 2, 2)), dma((2, 2, 2)),
            dma((2,)), dma((2,)), dma((2, nx)), dma((2, nx)), dma((2, nx)), dma((2, nx)),
            dma((2, nx)), dma((2, nx)), dma((3,)), dma((3,)), dma((3, nx)), dma((3, nx)),
        ],
        compiler_params=pltpu.CompilerParams(
            collective_id=0, has_side_effects=True, vmem_limit_bytes=62200 * 1024
        ),
        name="demons",
    )(
        images, velocity, weights, template.reshape(rows * pd, LANES),
        jnp.swapaxes(owners, 1, 2), local_rows, tile_counts.T,
    )
    return field, planes.reshape(template.shape)


def solution(mesh):
    nj, ns = mesh.shape["subj"], mesh.shape["space"]
    nz = 8 if ns % 8 == 0 else 2
    in_specs = (
        P("subj", "space", None, None),
        P(None, "subj", "space", None, None),
        P(None, "subj", "space", None, None),
        P("space", "subj", None),
        P("subj", "space", None),
        P("subj", "space"),
        P("subj", "space"),
    )
    out_specs = (P(None, "subj", "space", None, None), P("space", "subj", None))
    return jax.shard_map(
        functools.partial(body, nj, ns // nz, nz),
        mesh=mesh, in_specs=in_specs, out_specs=out_specs, check_vma=False,
    )
```
